128 devices in a mesh: nodes: 128 (over z, y, x, core).
Axes of the slice: x: 4, y: 4, z: 4, core: 2. Of those that a mesh axis runs over, the one named last changes fastest.
Arguments:
- features: float32 [131072, 768], P('nodes'), may hold values from -6 to 6
- history: float32 [131072, 256], P('nodes'), may hold values from -6 to 6
- request_ids: int32 [128, 128, 16], P('nodes'), may hold values from 0 to 1023
- request_count: int32 [128, 128], P('nodes'), may hold values from 1 to 16, as said below
- halo_ids: int32 [128, 128, 8], P('nodes'), may hold values from 0 to 1023
- halo_count: int32 [128, 128], P('nodes'), may hold values from 1 to 8, as said below
- tile_values: bfloat16 [65536, 128, 128], P('nodes'), may hold values from -0.25 to 0.25
- tile_rows: int32 [65536], P('nodes'), may hold values from 0 to 15
- tile_cols: int32 [65536], P('nodes'), may hold values from 0 to 23
- tile_count: int32 [128], P('nodes'), may hold values from 1 to 512, as said below
- w_in: bfloat16 [768, 256], replicated, may hold values from -0.21875 to 0.21875
- w_out: bfloat16 [256, 256], replicated, may hold values from -0.375 to 0.375
Outputs:
- updated: bfloat16 [262144, 256], P('nodes')
The draws below stay inside these ranges and needn't reach their ends.
Inputs may be any that keep to these rules, and one draw needn't show every extreme that they name: `request_ids`: slots at or beyond the count are ignored. `request_count`: every cluster fills all 16 slots for some owner, and some owner receives full lists from every cluster. `halo_ids`: slots at or beyond the count are ignored. `halo_count`: every cluster fills all 8 slots for some owner, and some owner receives full lists from every cluster. `tile_count`: some cluster uses all 512 tile slots.
All inputs are finite; a program needn't handle non-finite values.
Results may differ from the reference program's by a relative error of at most 0.0059.
Values may be sent and summed in bfloat16 or wider, within the bound.
No kernel may reach another device: no remote copies, remote signals or barrier semaphores. Data moves between devices by JAX's collectives and lax.ppermute only.
A program may use at most 128 MiB of HBM per device.

```python
import jax
import jax.numpy as jnp
from jax import lax

D_IN = 768
D_HID = 256
ROWS_DEV = 1024
CLUSTER = 2048
HALO = 1024
TILE = 128
TD = 512
GROUP = 64
REQ = 16
HREQ = 8
N_NODES = 128


def capped_counts(key, owner_total, most_count):
    keys = jax.random.split(key, 4)
    base_count = jax.random.randint(keys[0], (owner_total, owner_total), 1, most_count + 1)
    hot_owner = jax.random.randint(keys[1], (owner_total,), 0, 4) == 0
    chosen = jax.random.randint(keys[2], (), 0, owner_total)
    owner_list = jnp.arange(owner_total)
    hot_owner = hot_owner | (owner_list == chosen)
    full_owner = jax.random.randint(keys[3], (owner_total,), 0, owner_total)
    is_full = hot_owner[None, :] | (owner_list[None, :] == full_owner[:, None])
    return jnp.where(is_full, most_count, base_count).astype(jnp.int32)


def draw_request_count(key, part):
    return capped_counts(jax.random.fold_in(key, 11), N_NODES, REQ)


def draw_halo_count(key, part):
    return capped_counts(jax.random.fold_in(key, 23), N_NODES, HREQ)


def draw_tile_count(key, part):
    keys = jax.random.split(jax.random.fold_in(key, 37), 2)
    base_count = jax.random.randint(keys[0], (N_NODES,), max(1, TD // 4), TD + 1)
    chosen = jax.random.randint(keys[1], (), 0, N_NODES)
    return jnp.where(jnp.arange(N_NODES) == chosen, TD, base_count).astype(jnp.int32)


def plant(entries, rng, low, high):
    dims = entries.shape
    spot = [jax.random.randint(jax.random.fold_in(rng, axis), (), 0, dims[axis]) for axis in range(len(dims))]
    entries = entries.at[tuple(spot)].set(low)
    longest = dims.index(max(dims))
    spot[longest] = (spot[longest] + 1) % dims[longest]
    return entries.at[tuple(spot)].set(high)


def levels(key, dims, cuts, smallest, top_value):
    loudness = 1.0
    for dim, parts in cuts:
        draws = jax.random.uniform(jax.random.fold_in(jax.random.fold_in(key, 6), dim), (parts,), jnp.float32, smallest / len(cuts), top_value / len(cuts))
        loudness = loudness * jnp.repeat(jnp.exp(draws), dims[dim] // parts).reshape((-1,) + (1,) * (len(dims) - 1 - dim))
    return loudness


def centred(stream_key, dims, width, most, cuts=(), kind=jnp.bfloat16):
    values = jax.random.normal(stream_key, dims, jnp.float32) * width
    if len(cuts) > 0:
        values = levels(stream_key, dims, cuts, -0.22, 0.18) * values
    return jnp.clip(values, min=-most, max=most).astype(kind)


def setup_inputs(seed: int = 0) -> dict:
    splits = jax.random.split(jax.random.key(seed), 13)
    features = centred(splits[0], (N_NODES * ROWS_DEV, D_IN), 1.0, 6.0, ((0, 128),), jnp.float32)
    history = centred(splits[1], (N_NODES * ROWS_DEV, D_HID), 1.0, 6.0, ((0, 128),), jnp.float32)
    request_ids = plant(jax.random.randint(splits[2], (N_NODES, N_NODES, REQ), 0, ROWS_DEV), jax.random.fold_in(splits[2], 1), 0, ROWS_DEV - 1).astype(jnp.int32)
    request_count = draw_request_count(jax.random.fold_in(splits[12], 71), 0)
    halo_ids = plant(jax.random.randint(splits[4], (N_NODES, N_NODES, HREQ), 0, ROWS_DEV), jax.random.fold_in(splits[4], 1), 0, ROWS_DEV - 1).astype(jnp.int32)
    halo_count = draw_halo_count(jax.random.fold_in(splits[12], 71), 0)
    tile_values = centred(splits[6], (N_NODES * TD, TILE, TILE), ((CLUSTER / (TD * TILE * TILE)) ** 0.5), 0.25, ((0, 128),))
    tile_rows = plant(jax.random.randint(splits[7], (N_NODES * TD,), 0, CLUSTER // TILE), jax.random.fold_in(splits[7], 1), 0, (CLUSTER // TILE) - 1).astype(jnp.int32)
    tile_cols = plant(jax.random.randint(splits[8], (N_NODES * TD,), 0, (CLUSTER + HALO) // TILE), jax.random.fold_in(splits[8], 1), 0, ((CLUSTER + HALO) // TILE) - 1).astype(jnp.int32)
    tile_count = draw_tile_count(jax.random.fold_in(splits[12], 71), 0)
    w_in = centred(splits[10], (D_IN, D_HID), D_IN ** -0.5, 0.21875)
    w_out = centred(splits[11], (D_HID, D_HID), D_HID ** -0.5, 0.375)
    return dict(features=features, history=history, request_ids=request_ids, request_count=request_count, halo_ids=halo_ids, halo_count=halo_count, tile_values=tile_values, tile_rows=tile_rows, tile_cols=tile_cols, tile_count=tile_count, w_in=w_in, w_out=w_out)


def aggregate(source, tile_block, row_list, col_list, used):
    row_blocks = CLUSTER // TILE
    blocks = source.reshape(-1, TILE, D_HID)

    def add_group(running, group_index):
        start = group_index * GROUP
        vals_group = lax.dynamic_slice_in_dim(tile_block, start, GROUP, 0)
        rows_group = lax.dynamic_slice_in_dim(row_list, start, GROUP, 0)
        cols_group = lax.dynamic_slice_in_dim(col_list, start, GROUP, 0)
        picked = blocks[cols_group]
        products = jnp.einsum("gij,gjk->gik", vals_group.astype(jnp.float32), picked.astype(jnp.float32), precision=lax.Precision.HIGHEST)
        order = start + jnp.arange(GROUP, dtype=jnp.int32)
        row_match = ((rows_group[None, :] == jnp.arange(row_blocks, dtype=jnp.int32)[:, None]) & (order[None, :] < used)).astype(jnp.float32)
        running = running + jnp.dot(row_match, products.reshape(GROUP, -1), precision=lax.Precision.HIGHEST)
        return running, None

    start_sum = jnp.zeros((row_blocks, TILE * D_HID), jnp.float32)
    total, _ = lax.scan(add_group, start_sum, jnp.arange(TD // GROUP, dtype=jnp.int32))
    return total.reshape(CLUSTER, D_HID)


def reference(features, history, request_ids, request_count, halo_ids, halo_count, tile_values, tile_rows, tile_cols, tile_count, w_in, w_out):
    owner_base = jnp.arange(N_NODES, dtype=jnp.int32)[:, None] * ROWS_DEV

    def one_cluster(pieces):
        wanted, wanted_count, halo_wanted, halo_wanted_count, tile_block, row_list, col_list, used = pieces
        index_list = (owner_base + wanted).reshape(-1)
        is_live = (jnp.arange(REQ, dtype=jnp.int32)[None, :] < wanted_count[:, None]).reshape(-1, 1)
        requested = jnp.where(is_live, features[index_list], 0.0).astype(jnp.bfloat16)
        projected = jnp.dot(requested, w_in, preferred_element_type=jnp.float32).astype(jnp.bfloat16)
        halo_index = (owner_base + halo_wanted).reshape(-1)
        halo_live = (jnp.arange(HREQ, dtype=jnp.int32)[None, :] < halo_wanted_count[:, None]).reshape(-1, 1)
        halo_rows = jnp.where(halo_live, history[halo_index], 0.0).astype(jnp.bfloat16)
        source = jnp.concatenate([projected, halo_rows], axis=0)
        aggregated = aggregate(source, tile_block, row_list, col_list, used).astype(jnp.bfloat16)
        mixed = jnp.dot(aggregated, w_out, preferred_element_type=jnp.float32) + projected.astype(jnp.float32)
        return jax.nn.relu(mixed).astype(jnp.bfloat16)

    stacked = (request_ids, request_count, halo_ids, halo_count,
               tile_values.reshape(N_NODES, TD, TILE, TILE),
               tile_rows.reshape(N_NODES, TD), tile_cols.reshape(N_NODES, TD), tile_count)
    updated = lax.map(one_cluster, stacked)
    return updated.reshape(N_NODES * CLUSTER, D_HID)
```

```python
import functools

import jax
import jax.numpy as jnp
from jax import lax
from jax.experimental import pallas as pl
from jax.experimental.pallas import tpu as pltpu
from jax.sharding import PartitionSpec as P

LANES = 128
TILE_STEP = 32
OWNERS_STEP = 16
ROWS_STEP = 512


def pack_kernel(req_ref, halo_ref, req_count_ref, halo_count_ref, out_ref):
    req = req_ref[...]
    halo = halo_ref[...]
    req_slot = lax.broadcasted_iota(jnp.int32, req.shape, 0)
    halo_slot = lax.broadcasted_iota(jnp.int32, halo.shape, 0)
    req = jnp.where(req_slot < req_count_ref[...], req, -1)
    halo = jnp.where(halo_slot < halo_count_ref[...], halo, -1)
    rest = jnp.full((LANES - req.shape[0] - halo.shape[0], req.shape[1]), -1, jnp.int32)
    out_ref[...] = jnp.concatenate([req, halo, rest], axis=0).T


def pack_ids(req_t, halo_t, req_count, halo_count):
    owners = req_t.shape[1]
    return pl.pallas_call(
        pack_kernel,
        out_shape=jax.ShapeDtypeStruct((owners, LANES), jnp.int32),
        name="pack_ids",
    )(req_t, halo_t, req_count, halo_count)


def pick_kernel(req, halo, ids_ref, proj_ref, hist_ref, out_ref, turned_ref):
    count = ids_ref.shape[0]
    rows = proj_ref.shape[0]
    turned_ref[...] = ids_ref[...].T[: req + halo]
    group = OWNERS_STEP

    def one_hot(columns, start, size):
        wanted = jnp.concatenate(
            [columns[start : start + size, j : j + 1] for j in range(group)], axis=0
        )
        wide = jnp.broadcast_to(wanted, (size * group, LANES))
        lane = lax.broadcasted_iota(jnp.int32, wide.shape, 1)
        parts = [
            jnp.where(wide == lane + k * LANES, 1.0, 0.0).astype(jnp.bfloat16)
            for k in range(rows // LANES)
        ]
        return jnp.concatenate(parts, axis=1)

    @pl.loop(0, count // group)
    def _(g):
        columns = pltpu.roll(turned_ref[...], lax.rem(count - g * group, count), 1)
        at = pl.ds(g * group, group)
        picked = jnp.dot(
            one_hot(columns, 0, req), proj_ref[...], preferred_element_type=jnp.float32
        ).astype(jnp.bfloat16)
        out_ref[at, :req, :] = picked.reshape(group, req, -1)
        picked = jnp.dot(
            one_hot(columns, req, halo), hist_ref[...], preferred_element_type=jnp.float32
        ).astype(jnp.bfloat16)
        out_ref[at, req:, :] = picked.reshape(group, halo, -1)


def pick_rows(ids, proj, hist, req, halo):
    count = ids.shape[0]
    hidden = proj.shape[1]
    flops = 2 * count * (req + halo) * proj.shape[0] * hidden
    return pl.pallas_call(
        functools.partial(pick_kernel, req, halo),
        out_shape=jax.ShapeDtypeStruct((count, req + halo, hidden), jnp.bfloat16),
        scratch_shapes=[pltpu.VMEM((req + halo, count), jnp.int32)],
        cost_estimate=pl.CostEstimate(flops=flops, bytes_accessed=3 << 20, transcendentals=0),
        name="pick_rows",
    )(ids, proj, hist)


def dense_kernel(col_blocks, fill_steps, rows_ref, cols_ref, used_ref, tiles_ref, out_ref, acc_ref):
    i = pl.program_id(0)
    side = tiles_ref.shape[1]

    @pl.when(i == 0)
    def _():
        @pl.loop(0, acc_ref.shape[0])
        def _(b):
            acc_ref[b] = jnp.zeros(acc_ref.shape[1:], jnp.float32)

    @pl.when(i < fill_steps)
    def _():
        first = i * TILE_STEP
        live = jnp.clip(used_ref[0] - first, 0, TILE_STEP)

        @pl.loop(0, live)
        def _(t):
            block = rows_ref[first + t] * col_blocks + cols_ref[first + t]
            acc_ref[block] = acc_ref[block] + tiles_ref[t].astype(jnp.float32)

    @pl.when(i >= fill_steps)
    def _():
        base = (i - fill_steps) * col_blocks
        for c in range(col_blocks):
            out_ref[:, c * side : (c + 1) * side] = acc_ref[base + c].astype(jnp.bfloat16)


def build_dense(tile_rows, tile_cols, tile_count, tile_values, row_blocks, col_blocks):
    slots, side, _ = tile_values.shape
    fill_steps = slots // TILE_STEP
    last = fill_steps - 1
    return pl.pallas_call(
        functools.partial(dense_kernel, col_blocks, fill_steps),
        grid_spec=pltpu.PrefetchScalarGridSpec(
            num_scalar_prefetch=3,
            grid=(fill_steps + row_blocks,),
            in_specs=[
                pl.BlockSpec(
                    (TILE_STEP, side, side), lambda i, *_: (jnp.minimum(i, last), 0, 0)
                )
            ],
            out_specs=pl.BlockSpec(
                (side, col_blocks * side), lambda i, *_: (jnp.maximum(i - fill_steps, 0), 0)
            ),
            scratch_shapes=[pltpu.VMEM((row_blocks * col_blocks, side, side), jnp.float32)],
        ),
        out_shape=jax.ShapeDtypeStruct((row_blocks * side, col_blocks * side), jnp.bfloat16),
        compiler_params=pltpu.CompilerParams(vmem_limit_bytes=36 << 20),
        cost_estimate=pl.CostEstimate(flops=1 << 20, bytes_accessed=30 << 20, transcendentals=0),
        name="build_dense",
    )(tile_rows, tile_cols, tile_count, tile_values)


def combine_kernel(req, dense_ref, came_ref, w_ref, out_ref, source_ref):
    i = pl.program_id(0)
    owners, slots, hidden = came_ref.shape
    nodes = owners * req

    @pl.when(i == 0)
    def _():
        source_ref[:nodes] = came_ref[:, :req, :].reshape(nodes, hidden)
        source_ref[nodes:] = came_ref[:, req:, :].reshape(owners * (slots - req), hidden)

    total = jnp.dot(dense_ref[...], source_ref[...], preferred_element_type=jnp.float32)
    mixed = jnp.dot(total.astype(jnp.bfloat16), w_ref[...], preferred_element_type=jnp.float32)
    own = source_ref[pl.ds(i * out_ref.shape[0], out_ref.shape[0]), :].astype(jnp.float32)
    out_ref[...] = jnp.maximum(mixed + own, 0.0).astype(jnp.bfloat16)


def combine(dense, came, w_out, req):
    owners, slots, hidden = came.shape
    nodes, width = dense.shape
    step = ROWS_STEP
    return pl.pallas_call(
        functools.partial(combine_kernel, req),
        grid=(nodes // step,),
        in_specs=[
            pl.BlockSpec((step, width), lambda i: (i, 0)),
            pl.BlockSpec((owners, slots, hidden), lambda i: (0, 0, 0)),
            pl.BlockSpec((hidden, hidden), lambda i: (0, 0)),
        ],
        out_specs=pl.BlockSpec((step, hidden), lambda i: (i, 0)),
        out_shape=jax.ShapeDtypeStruct((nodes, hidden), jnp.bfloat16),
        scratch_shapes=[pltpu.VMEM((width, hidden), jnp.bfloat16)],
        cost_estimate=pl.CostEstimate(
            flops=2 * nodes * width * hidden, bytes_accessed=16 << 20, transcendentals=0
        ),
        compiler_params=pltpu.CompilerParams(vmem_limit_bytes=24 << 20),
        name="combine",
    )(dense, came, w_out)


def on_device(
    features,
    history,
    request_ids,
    request_count,
    halo_ids,
    halo_count,
    tile_values,
    tile_rows,
    tile_cols,
    tile_count,
    w_in,
    w_out,
):
    owners, req = request_ids.shape[1:]
    halo = halo_ids.shape[2]
    side = tile_values.shape[1]
    wanted = pack_ids(request_ids[0].T, halo_ids[0].T, request_count, halo_count)
    asked = lax.all_to_all(wanted, "nodes", split_axis=0, concat_axis=0, tiled=True)
    proj = jnp.dot(
        features.astype(jnp.bfloat16), w_in, preferred_element_type=jnp.float32
    ).astype(jnp.bfloat16)
    picked = pick_rows(asked, proj, history.astype(jnp.bfloat16), req, halo)
    picked, tile_count = lax.optimization_barrier((picked, tile_count))
    came = lax.all_to_all(picked, "nodes", split_axis=0, concat_axis=0, tiled=True)
    dense = build_dense(
        tile_rows, tile_cols, tile_count, tile_values,
        owners * req // side, owners * (req + halo) // side,
    )
    return combine(dense, came, w_out, req)


def solution(mesh):
    in_specs = (
        P("nodes", None),
        P("nodes", None),
        P("nodes", None, None),
        P("nodes", None),
        P("nodes", None, None),
        P("nodes", None),
        P("nodes", None, None),
        P("nodes"),
        P("nodes"),
        P("nodes"),
        P(),
        P(),
    )
    out_specs = P("nodes", None)
    return jax.shard_map(
        on_device, mesh=mesh, in_specs=in_specs, out_specs=out_specs, check_vma=False
    )
```

```python
import functools

import jax
import jax.numpy as jnp
from jax import lax
from jax.experimental import pallas as pl
from jax.experimental.pallas import tpu as pltpu
from jax.sharding import PartitionSpec as P

LANES = 128
TILE_CHUNKS = 8
TILE_UNROLL = 4
OUT_SLOTS = 8
PICK_PARTS = 2
ROWS_STEP = 512
PROJECT_STEP = 256


def pack_kernel(req_ref, halo_ref, req_count_ref, halo_count_ref, out_ref):
    req = req_ref[...]
    halo = halo_ref[...]
    req_slot = lax.broadcasted_iota(jnp.int32, req.shape, 0)
    halo_slot = lax.broadcasted_iota(jnp.int32, halo.shape, 0)
    req = jnp.where(req_slot < req_count_ref[...], req, -1)
    halo = jnp.where(halo_slot < halo_count_ref[...], halo, -1)
    rest = jnp.full((LANES - req.shape[0] - halo.shape[0], req.shape[1]), -1, jnp.int32)
    out_ref[...] = jnp.concatenate([req, halo, rest], axis=0).T


def pack_ids(req_t, halo_t, req_count, halo_count):
    owners = req_t.shape[1]
    return pl.pallas_call(
        pack_kernel,
        out_shape=jax.ShapeDtypeStruct((owners, LANES), jnp.int32),
        name="pack_ids",
    )(req_t, halo_t, req_count, halo_count)


def project_kernel(
    features_ref, history_ref, w_ref, proj_ref, hist_ref, rows_ref, old_ref, row_sem, old_sem
):
    step = PROJECT_STEP
    steps = proj_ref.shape[0] // step

    def fetch(k):
        at = pl.ds(k * step, step)
        return pltpu.make_async_copy(features_ref.at[at], rows_ref.at[at], row_sem.at[k])

    old = pltpu.make_async_copy(history_ref, old_ref, old_sem)
    for k in range(steps):
        fetch(k).start()
    old.start()

    @pl.loop(0, steps)
    def _(k):
        fetch(k).wait()
        at = pl.ds(pl.multiple_of(k * step, step), step)
        proj_ref[at] = jnp.dot(
            rows_ref[at].astype(jnp.bfloat16), w_ref[...], preferred_element_type=jnp.float32
        ).astype(jnp.bfloat16)

    old.wait()
    hist_ref[...] = old_ref[...].astype(jnp.bfloat16)


def project(features, history, w_in):
    rows, width = features.shape
    hidden = w_in.shape[1]
    table = jax.ShapeDtypeStruct((rows, hidden), jnp.bfloat16)
    vmem = pl.BlockSpec(memory_space=pltpu.VMEM)
    hbm = pl.BlockSpec(memory_space=pltpu.HBM)
    return pl.pallas_call(
        project_kernel,
        in_specs=[hbm, hbm, vmem],
        out_specs=[vmem, vmem],
        out_shape=[table, table],
        scratch_shapes=[
            pltpu.VMEM((rows, width), jnp.float32),
            pltpu.VMEM((rows, hidden), jnp.float32),
            pltpu.SemaphoreType.DMA((rows // PROJECT_STEP,)),
            pltpu.SemaphoreType.DMA,
        ],
        cost_estimate=pl.CostEstimate(
            flops=2 * rows * width * hidden, bytes_accessed=5 << 20, transcendentals=0
        ),
        compiler_params=pltpu.CompilerParams(vmem_limit_bytes=60 << 20),
        name="project",
    )(features, history, w_in)


def pick_kernel(req, halo, ids_ref, proj_ref, hist_ref, out_ref, req_ref, halo_ref, sem):
    count = ids_ref.shape[0]
    rows = proj_ref.shape[0]
    turned = ids_ref[...].T

    def pick(table_ref, start, size, first, last):
        wide = jnp.concatenate(
            [
                jnp.broadcast_to(turned[start : start + size, c : c + 1], (size, LANES))
                for c in range(first, last)
            ],
            axis=0,
        )
        high = (wide >> 7).astype(jnp.float32).astype(jnp.bfloat16)
        low = (wide & (LANES - 1)).astype(jnp.float32).astype(jnp.bfloat16)
        lane = lax.broadcasted_iota(jnp.int32, wide.shape, 1)
        lane = lane.astype(jnp.float32).astype(jnp.bfloat16)
        one, zero = jnp.ones_like(low), jnp.zeros_like(low)
        hit = jnp.where(low == lane, one, zero)
        parts = [
            jnp.where(high == jnp.full_like(high, k), hit, zero) for k in range(rows // LANES)
        ]
        picked = jnp.dot(
            jnp.concatenate(parts, axis=1), table_ref[...], preferred_element_type=jnp.float32
        )
        return picked.astype(jnp.bfloat16).reshape(last - first, size, -1)

    copies = []

    def send(held_ref, start, size, first, last):
        copy = pltpu.make_async_copy(
            held_ref.at[first:last],
            out_ref.at[first:last, start : start + size, :],
            sem.at[len(copies)],
        )
        copy.start()
        copies.append(copy)

    halo_ref[...] = pick(hist_ref, req, halo, 0, count)
    send(halo_ref, req, halo, 0, count)
    part = count // PICK_PARTS
    for first in range(0, count, part):
        req_ref[first : first + part] = pick(proj_ref, 0, req, first, first + part)
        send(req_ref, 0, req, first, first + part)
    for copy in copies:
        copy.wait()


def pick_rows(ids, proj, hist, req, halo):
    count = ids.shape[0]
    hidden = proj.shape[1]
    flops = 2 * count * (req + halo) * proj.shape[0] * hidden
    vmem = pl.BlockSpec(memory_space=pltpu.VMEM)
    return pl.pallas_call(
        functools.partial(pick_kernel, req, halo),
        in_specs=[vmem, vmem, vmem],
        out_specs=pl.BlockSpec(memory_space=pltpu.HBM),
        out_shape=jax.ShapeDtypeStruct((count, req + halo, hidden), jnp.bfloat16),
        scratch_shapes=[
            pltpu.VMEM((count, req, hidden), jnp.bfloat16),
            pltpu.VMEM((count, halo, hidden), jnp.bfloat16),
            pltpu.SemaphoreType.DMA((1 + PICK_PARTS,)),
        ],
        cost_estimate=pl.CostEstimate(flops=flops, bytes_accessed=3 << 20, transcendentals=0),
        compiler_params=pltpu.CompilerParams(vmem_limit_bytes=24 << 20),
        name="pick_rows",
    )(ids, proj, hist)


def dense_kernel(
    rows_ref, cols_ref, used_ref, tiles_ref, out_ref,
    held_ref, acc_ref, stage_ref, in_sem, out_sem,
):
    slots, side, _ = tiles_ref.shape
    blocks = acc_ref.shape[0] - 1
    row_blocks, width = out_ref.shape[0] // side, out_ref.shape[1]
    col_blocks = width // side
    chunk = slots // TILE_CHUNKS

    def fetch(c):
        at = pl.ds(c * chunk, chunk)
        return pltpu.make_async_copy(tiles_ref.at[at], held_ref.at[at], in_sem.at[c])

    def flush(r, slot):
        return pltpu.make_async_copy(
            stage_ref.at[slot], out_ref.at[pl.ds(r * side, side)], out_sem.at[slot]
        )

    for c in range(TILE_CHUNKS):
        fetch(c).start()

    @pl.loop(0, blocks)
    def _(b):
        acc_ref[b] = jnp.zeros(acc_ref.shape[1:], jnp.float32)

    @pl.loop(0, TILE_CHUNKS)
    def _(c):
        fetch(c).wait()

        live = jnp.clip(used_ref[0] - c * chunk, 0, chunk)

        @pl.loop(0, (live + TILE_UNROLL - 1) // TILE_UNROLL)
        def _(g):
            for u in range(TILE_UNROLL):
                t = c * chunk + g * TILE_UNROLL + u
                block = rows_ref[t] * col_blocks + cols_ref[t]
                block = jnp.where(t < used_ref[0], block, blocks)
                acc_ref[block] = acc_ref[block] + held_ref[t].astype(jnp.float32)

    @pl.loop(0, row_blocks)
    def _(r):
        slot = lax.rem(r, OUT_SLOTS)

        @pl.when(r >= OUT_SLOTS)
        def _():
            flush(r - OUT_SLOTS, slot).wait()

        for k in range(col_blocks):
            stage_ref[slot, :, k * side : (k + 1) * side] = acc_ref[r * col_blocks + k].astype(
                jnp.bfloat16
            )
        flush(r, slot).start()

    for r in range(row_blocks - OUT_SLOTS, row_blocks):
        flush(r, r % OUT_SLOTS).wait()


def build_dense(tile_rows, tile_cols, tile_count, tile_values, row_blocks, col_blocks):
    slots, side, _ = tile_values.shape
    smem = pl.BlockSpec(memory_space=pltpu.SMEM)
    hbm = pl.BlockSpec(memory_space=pltpu.HBM)
    return pl.pallas_call(
        dense_kernel,
        in_specs=[smem, smem, smem, hbm],
        out_specs=hbm,
        out_shape=jax.ShapeDtypeStruct((row_blocks * side, col_blocks * side), jnp.bfloat16),
        scratch_shapes=[
            pltpu.VMEM((slots, side, side), jnp.bfloat16),
            pltpu.VMEM((row_blocks * col_blocks + 1, side, side), jnp.float32),
            pltpu.VMEM((OUT_SLOTS, side, col_blocks * side), jnp.bfloat16),
            pltpu.SemaphoreType.DMA((TILE_CHUNKS,)),
            pltpu.SemaphoreType.DMA((OUT_SLOTS,)),
        ],
        compiler_params=pltpu.CompilerParams(vmem_limit_bytes=56 << 20),
        cost_estimate=pl.CostEstimate(flops=1 << 20, bytes_accessed=30 << 20, transcendentals=0),
        name="build_dense",
    )(tile_rows, tile_cols, tile_count, tile_values)


def combine_kernel(
    req, dense_ref, came_ref, w_ref, out_ref, held_ref, source_ref, stage_ref, in_sem, out_sem
):
    owners, slots, hidden = came_ref.shape
    nodes = owners * req
    step = ROWS_STEP
    steps = nodes // step

    def fetch(k):
        at = pl.ds(k * step, step)
        return pltpu.make_async_copy(dense_ref.at[at], held_ref.at[at], in_sem.at[k])

    def flush(k):
        at = pl.ds(k * step, step)
        return pltpu.make_async_copy(stage_ref.at[at], out_ref.at[at], out_sem.at[k])

    for k in range(2):
        fetch(k).start()
    source_ref[:nodes] = came_ref[:, :req, :].reshape(nodes, hidden)
    source_ref[nodes:] = came_ref[:, req:, :].reshape(owners * (slots - req), hidden)

    @pl.loop(0, steps)
    def _(k):
        fetch(k).wait()

        @pl.when(k + 2 < steps)
        def _():
            fetch(k + 2).start()

        at = pl.ds(pl.multiple_of(k * step, step), step)
        total = jnp.dot(held_ref[at], source_ref[...], preferred_element_type=jnp.float32)
        mixed = jnp.dot(total.astype(jnp.bfloat16), w_ref[...], preferred_element_type=jnp.float32)
        own = source_ref[at].astype(jnp.float32)
        stage_ref[at] = jnp.maximum(mixed + own, 0.0).astype(jnp.bfloat16)
        flush(k).start()

    for k in range(steps):
        flush(k).wait()


def combine(dense, came, w_out, req):
    hidden = came.shape[2]
    nodes, width = dense.shape
    vmem = pl.BlockSpec(memory_space=pltpu.VMEM)
    hbm = pl.BlockSpec(memory_space=pltpu.HBM)
    return pl.pallas_call(
        functools.partial(combine_kernel, req),
        in_specs=[hbm, vmem, vmem],
        out_specs=hbm,
        out_shape=jax.ShapeDtypeStruct((nodes, hidden), jnp.bfloat16),
        scratch_shapes=[
            pltpu.VMEM((nodes, width), jnp.bfloat16),
            pltpu.VMEM((width, hidden), jnp.bfloat16),
            pltpu.VMEM((nodes, hidden), jnp.bfloat16),
            pltpu.SemaphoreType.DMA((nodes // ROWS_STEP,)),
            pltpu.SemaphoreType.DMA((nodes // ROWS_STEP,)),
        ],
        cost_estimate=pl.CostEstimate(
            flops=2 * nodes * width * hidden, bytes_accessed=16 << 20, transcendentals=0
        ),
        compiler_params=pltpu.CompilerParams(vmem_limit_bytes=52 << 20),
        name="combine",
    )(dense, came, w_out)


def on_device(
    features,
    history,
    request_ids,
    request_count,
    halo_ids,
    halo_count,
    tile_values,
    tile_rows,
    tile_cols,
    tile_count,
    w_in,
    w_out,
):
    owners, req = request_ids.shape[1:]
    halo = halo_ids.shape[2]
    side = tile_values.shape[1]
    wanted = pack_ids(request_ids[0].T, halo_ids[0].T, request_count, halo_count)
    asked = lax.all_to_all(wanted, "nodes", split_axis=0, concat_axis=0, tiled=True)
    proj, hist = project(features, history, w_in)
    picked = pick_rows(asked, proj, hist, req, halo)
    picked, tile_count = lax.optimization_barrier((picked, tile_count))
    came = lax.all_to_all(picked, "nodes", split_axis=0, concat_axis=0, tiled=True)
    dense = build_dense(
        tile_rows, tile_cols, tile_count, tile_values,
        owners * req // side, owners * (req + halo) // side,
    )
    return combine(dense, came, w_out, req)


def solution(mesh):
    in_specs = (
        P("nodes", None),
        P("nodes", None),
        P("nodes", None, None),
        P("nodes", None),
        P("nodes", None, None),
        P("nodes", None),
        P("nodes", None, None),
        P("nodes"),
        P("nodes"),
        P("nodes"),
        P(),
        P(),
    )
    out_specs = P("nodes", None)
    return jax.shard_map(
        on_device, mesh=mesh, in_specs=in_specs, out_specs=out_specs, check_vma=False
    )
```

```python
import functools

import jax
import jax.numpy as jnp
from jax import lax
from jax.experimental import pallas as pl
from jax.experimental.pallas import tpu as pltpu
from jax.sharding import PartitionSpec as P

LANES = 128
TILE_CHUNKS = 8
TILE_UNROLL = 4
OUT_SLOTS = 8
PICK_PARTS = 2
ROWS_STEP = 512
KEPT_ROWS = 256
PROJECT_STEP = 512


def pack_kernel(req_ref, halo_ref, req_count_ref, halo_count_ref, out_ref):
    req = req_ref[...]
    halo = halo_ref[...]
    req_slot = lax.broadcasted_iota(jnp.int32, req.shape, 0)
    halo_slot = lax.broadcasted_iota(jnp.int32, halo.shape, 0)
    req = jnp.where(req_slot < req_count_ref[...], req, -1)
    halo = jnp.where(halo_slot < halo_count_ref[...], halo, -1)
    rest = jnp.full((LANES - req.shape[0] - halo.shape[0], req.shape[1]), -1, jnp.int32)
    out_ref[...] = jnp.concatenate([req, halo, rest], axis=0).T


def pack_ids(req_t, halo_t, req_count, halo_count):
    owners = req_t.shape[1]
    return pl.pallas_call(
        pack_kernel,
        out_specs=pl.BlockSpec(memory_space=pltpu.VMEM),
        out_shape=pltpu.VMEM((owners, LANES), jnp.int32),
        name="pack_ids",
    )(req_t, halo_t, req_count, halo_count)


def project_kernel(
    features_ref, history_ref, w_ref, proj_ref, hist_ref, rows_ref, old_ref, row_sem, old_sem
):
    step = PROJECT_STEP
    steps = proj_ref.shape[0] // step

    def fetch(k):
        at = pl.ds(k * step, step)
        return pltpu.make_async_copy(features_ref.at[at], rows_ref.at[at], row_sem.at[k])

    old = pltpu.make_async_copy(history_ref, old_ref, old_sem)
    for k in range(steps):
        fetch(k).start()
    old.start()

    @pl.loop(0, steps)
    def _(k):
        fetch(k).wait()
        at = pl.ds(pl.multiple_of(k * step, step), step)
        proj_ref[at] = jnp.dot(
            rows_ref[at].astype(jnp.bfloat16), w_ref[...], preferred_element_type=jnp.float32
        ).astype(jnp.bfloat16)

    old.wait()
    hist_ref[...] = old_ref[...].astype(jnp.bfloat16)


def project(features, history, w_in):
    rows, width = features.shape
    hidden = w_in.shape[1]
    table = pltpu.VMEM((rows, hidden), jnp.bfloat16)
    features = pltpu.with_memory_space_constraint(features, pltpu.HBM)
    history = pltpu.with_memory_space_constraint(history, pltpu.HBM)
    vmem = pl.BlockSpec(memory_space=pltpu.VMEM)
    hbm = pl.BlockSpec(memory_space=pltpu.HBM)
    return pl.pallas_call(
        project_kernel,
        in_specs=[hbm, hbm, vmem],
        out_specs=[vmem, vmem],
        out_shape=[table, table],
        scratch_shapes=[
            pltpu.VMEM((rows, width), jnp.float32),
            pltpu.VMEM((rows, hidden), jnp.float32),
            pltpu.SemaphoreType.DMA((rows // PROJECT_STEP,)),
            pltpu.SemaphoreType.DMA,
        ],
        cost_estimate=pl.CostEstimate(
            flops=2 * rows * width * hidden, bytes_accessed=5 << 20, transcendentals=0
        ),
        compiler_params=pltpu.CompilerParams(vmem_limit_bytes=60 << 20),
        name="project",
    )(features, history, w_in)


def pick_kernel(req, halo, ids_ref, proj_ref, hist_ref, out_ref, req_ref, halo_ref, sem):
    count = ids_ref.shape[0]
    rows = proj_ref.shape[0]
    turned = ids_ref[...].T

    def pick(table_ref, start, size, first, last):
        wide = jnp.concatenate(
            [
                jnp.broadcast_to(turned[start : start + size, c : c + 1], (size, LANES))
                for c in range(first, last)
            ],
            axis=0,
        )
        high = (wide >> 7).astype(jnp.float32).astype(jnp.bfloat16)
        low = (wide & (LANES - 1)).astype(jnp.float32).astype(jnp.bfloat16)
        lane = lax.broadcasted_iota(jnp.int32, wide.shape, 1)
        lane = lane.astype(jnp.float32).astype(jnp.bfloat16)
        one, zero = jnp.ones_like(low), jnp.zeros_like(low)
        hit = jnp.where(low == lane, one, zero)
        parts = [
            jnp.where(high == jnp.full_like(high, k), hit, zero) for k in range(rows // LANES)
        ]
        picked = jnp.dot(
            jnp.concatenate(parts, axis=1), table_ref[...], preferred_element_type=jnp.float32
        )
        return picked.astype(jnp.bfloat16).reshape(last - first, size, -1)

    copies = []

    def send(held_ref, start, size, first, last):
        copy = pltpu.make_async_copy(
            held_ref.at[first:last],
            out_ref.at[first:last, start : start + size, :],
            sem.at[len(copies)],
        )
        copy.start()
        copies.append(copy)

    halo_ref[...] = pick(hist_ref, req, halo, 0, count)
    send(halo_ref, req, halo, 0, count)
    part = count // PICK_PARTS
    for first in range(0, count, part):
        req_ref[first : first + part] = pick(proj_ref, 0, req, first, first + part)
        send(req_ref, 0, req, first, first + part)
    for copy in copies:
        copy.wait()


def pick_rows(ids, proj, hist, req, halo):
    count = ids.shape[0]
    hidden = proj.shape[1]
    flops = 2 * count * (req + halo) * proj.shape[0] * hidden
    vmem = pl.BlockSpec(memory_space=pltpu.VMEM)
    return pl.pallas_call(
        functools.partial(pick_kernel, req, halo),
        in_specs=[vmem, vmem, vmem],
        out_specs=pl.BlockSpec(memory_space=pltpu.HBM),
        out_shape=jax.ShapeDtypeStruct((count, req + halo, hidden), jnp.bfloat16),
        scratch_shapes=[
            pltpu.VMEM((count, req, hidden), jnp.bfloat16),
            pltpu.VMEM((count, halo, hidden), jnp.bfloat16),
            pltpu.SemaphoreType.DMA((1 + PICK_PARTS,)),
        ],
        cost_estimate=pl.CostEstimate(flops=flops, bytes_accessed=3 << 20, transcendentals=0),
        compiler_params=pltpu.CompilerParams(vmem_limit_bytes=24 << 20),
        name="pick_rows",
    )(ids, proj, hist)


def dense_kernel(
    rows_ref, cols_ref, used_ref, tiles_ref, kept_ref, out_ref,
    held_ref, acc_ref, stage_ref, in_sem, out_sem,
):
    slots, side, _ = tiles_ref.shape
    blocks = acc_ref.shape[0] - 1
    kept_blocks = kept_ref.shape[0] // side
    row_blocks, width = out_ref.shape[0] // side, out_ref.shape[1]
    col_blocks = width // side
    chunk = slots // TILE_CHUNKS

    def fetch(c):
        at = pl.ds(c * chunk, chunk)
        return pltpu.make_async_copy(tiles_ref.at[at], held_ref.at[at], in_sem.at[c])

    def flush(r, slot):
        return pltpu.make_async_copy(
            stage_ref.at[slot], out_ref.at[pl.ds(r * side, side)], out_sem.at[slot]
        )

    for c in range(TILE_CHUNKS):
        fetch(c).start()

    @pl.loop(0, blocks)
    def _(b):
        acc_ref[b] = jnp.zeros(acc_ref.shape[1:], jnp.float32)

    @pl.loop(0, TILE_CHUNKS)
    def _(c):
        fetch(c).wait()

        live = jnp.clip(used_ref[0] - c * chunk, 0, chunk)

        @pl.loop(0, (live + TILE_UNROLL - 1) // TILE_UNROLL)
        def _(g):
            for u in range(TILE_UNROLL):
                t = c * chunk + g * TILE_UNROLL + u
                block = rows_ref[t] * col_blocks + cols_ref[t]
                block = jnp.where(t < used_ref[0], block, blocks)
                acc_ref[block] = acc_ref[block] + held_ref[t].astype(jnp.float32)

    @pl.loop(0, row_blocks)
    def _(r):
        slot = lax.rem(r, OUT_SLOTS)

        @pl.when(r >= OUT_SLOTS)
        def _():
            flush(r - OUT_SLOTS, slot).wait()

        for k in range(col_blocks):
            stage_ref[slot, :, k * side : (k + 1) * side] = acc_ref[
                (kept_blocks + r) * col_blocks + k
            ].astype(jnp.bfloat16)
        flush(r, slot).start()

    @pl.loop(0, kept_blocks)
    def _(r):
        at = pl.ds(pl.multiple_of(r * side, side), side)
        for k in range(col_blocks):
            kept_ref[at, k * side : (k + 1) * side] = acc_ref[r * col_blocks + k].astype(
                jnp.bfloat16
            )

    for r in range(row_blocks - OUT_SLOTS, row_blocks):
        flush(r, r % OUT_SLOTS).wait()


def build_dense(tile_rows, tile_cols, tile_count, tile_values, row_blocks, col_blocks):
    slots, side, _ = tile_values.shape
    width = col_blocks * side
    tile_values = pltpu.with_memory_space_constraint(tile_values, pltpu.HBM)
    smem = pl.BlockSpec(memory_space=pltpu.SMEM)
    hbm = pl.BlockSpec(memory_space=pltpu.HBM)
    return pl.pallas_call(
        dense_kernel,
        in_specs=[smem, smem, smem, hbm],
        out_specs=[pl.BlockSpec(memory_space=pltpu.VMEM), hbm],
        out_shape=[
            pltpu.VMEM((KEPT_ROWS, width), jnp.bfloat16),
            jax.ShapeDtypeStruct((row_blocks * side - KEPT_ROWS, width), jnp.bfloat16),
        ],
        scratch_shapes=[
            pltpu.VMEM((slots, side, side), jnp.bfloat16),
            pltpu.VMEM((row_blocks * col_blocks + 1, side, side), jnp.float32),
            pltpu.VMEM((OUT_SLOTS, side, col_blocks * side), jnp.bfloat16),
            pltpu.SemaphoreType.DMA((TILE_CHUNKS,)),
            pltpu.SemaphoreType.DMA((OUT_SLOTS,)),
        ],
        compiler_params=pltpu.CompilerParams(vmem_limit_bytes=56 << 20),
        cost_estimate=pl.CostEstimate(flops=1 << 20, bytes_accessed=30 << 20, transcendentals=0),
        name="build_dense",
    )(tile_rows, tile_cols, tile_count, tile_values)


def combine_kernel(
    req, kept_ref, dense_ref, came_ref, w_ref, out_ref,
    held_ref, source_ref, stage_ref, kept_sem, in_sem, out_sem,
):
    owners, slots, hidden = came_ref.shape
    nodes = owners * req
    step = ROWS_STEP
    steps = nodes // step

    kept = kept_ref.shape[0]

    def fetch(first, size, k):
        return pltpu.make_async_copy(
            dense_ref.at[pl.ds(first - kept, size)], held_ref.at[pl.ds(first, size)], in_sem.at[k]
        )

    def fetch_step(k):
        return fetch(k * step, step, k)

    near = pltpu.make_async_copy(kept_ref, held_ref.at[pl.ds(0, kept)], kept_sem)
    start = fetch(kept, step - kept, 0)

    def flush(k):
        at = pl.ds(k * step, step)
        return pltpu.make_async_copy(stage_ref.at[at], out_ref.at[at], out_sem.at[k])

    start.start()
    near.start()
    fetch_step(1).start()
    source_ref[:nodes] = came_ref[:, :req, :].reshape(nodes, hidden)
    source_ref[nodes:] = came_ref[:, req:, :].reshape(owners * (slots - req), hidden)

    @pl.loop(0, steps)
    def _(k):
        @pl.when(k == 0)
        def _():
            start.wait()
            near.wait()

        @pl.when(k > 0)
        def _():
            fetch_step(k).wait()

        @pl.when(k + 2 < steps)
        def _():
            fetch_step(k + 2).start()

        at = pl.ds(pl.multiple_of(k * step, step), step)
        total = jnp.dot(held_ref[at], source_ref[...], preferred_element_type=jnp.float32)
        mixed = jnp.dot(total.astype(jnp.bfloat16), w_ref[...], preferred_element_type=jnp.float32)
        own = source_ref[at].astype(jnp.float32)
        stage_ref[at] = jnp.maximum(mixed + own, 0.0).astype(jnp.bfloat16)
        flush(k).start()

    for k in range(steps):
        flush(k).wait()


def combine(kept, dense, came, w_out, req):
    hidden = came.shape[2]
    nodes, width = kept.shape[0] + dense.shape[0], dense.shape[1]
    dense = pltpu.with_memory_space_constraint(dense, pltpu.HBM)
    vmem = pl.BlockSpec(memory_space=pltpu.VMEM)
    hbm = pl.BlockSpec(memory_space=pltpu.HBM)
    return pl.pallas_call(
        functools.partial(combine_kernel, req),
        in_specs=[vmem, hbm, vmem, vmem],
        out_specs=hbm,
        out_shape=jax.ShapeDtypeStruct((nodes, hidden), jnp.bfloat16),
        scratch_shapes=[
            pltpu.VMEM((nodes, width), jnp.bfloat16),
            pltpu.VMEM((width, hidden), jnp.bfloat16),
            pltpu.VMEM((nodes, hidden), jnp.bfloat16),
            pltpu.SemaphoreType.DMA,
            pltpu.SemaphoreType.DMA((nodes // ROWS_STEP,)),
            pltpu.SemaphoreType.DMA((nodes // ROWS_STEP,)),
        ],
        cost_estimate=pl.CostEstimate(
            flops=2 * nodes * width * hidden, bytes_accessed=16 << 20, transcendentals=0
        ),
        compiler_params=pltpu.CompilerParams(vmem_limit_bytes=24 << 20),
        name="combine",
    )(kept, dense, came, w_out)


def on_device(
    features,
    history,
    request_ids,
    request_count,
    halo_ids,
    halo_count,
    tile_values,
    tile_rows,
    tile_cols,
    tile_count,
    w_in,
    w_out,
):
    owners, req = request_ids.shape[1:]
    halo = halo_ids.shape[2]
    side = tile_values.shape[1]
    wanted = pack_ids(request_ids[0].T, halo_ids[0].T, request_count, halo_count)
    asked = lax.all_to_all(wanted, "nodes", split_axis=0, concat_axis=0, tiled=True)
    proj, hist = project(features, history, w_in)
    picked = pick_rows(asked, proj, hist, req, halo)
    picked, tile_count = lax.optimization_barrier((picked, tile_count))
    came = lax.all_to_all(picked, "nodes", split_axis=0, concat_axis=0, tiled=True)
    kept, dense = build_dense(
        tile_rows, tile_cols, tile_count, tile_values,
        owners * req // side, owners * (req + halo) // side,
    )
    return combine(kept, dense, came, w_out, req)


def solution(mesh):
    in_specs = (
        P("nodes", None),
        P("nodes", None),
        P("nodes", None, None),
        P("nodes", None),
        P("nodes", None, None),
        P("nodes", None),
        P("nodes", None, None),
        P("nodes"),
        P("nodes"),
        P("nodes"),
        P(),
        P(),
    )
    out_specs = P("nodes", None)
    return jax.shard_map(
        on_device, mesh=mesh, in_specs=in_specs, out_specs=out_specs, check_vma=False
    )
```

```python
import functools

import jax
import jax.numpy as jnp
from jax import lax
from jax.experimental import pallas as pl
from jax.experimental.pallas import tpu as pltpu
from jax.sharding import PartitionSpec as P

LANES = 128
TILE_CHUNKS = 8
TILE_UNROLL = 4
OUT_SLOTS = 8
PICK_PARTS = 2
ROWS_STEP = 512
KEPT_ROWS = 256
PROJECT_STEP = 512


def pack_kernel(req_ref, halo_ref, req_count_ref, halo_count_ref, out_ref):
    req = req_ref[...]
    halo = halo_ref[...]
    req_slot = lax.broadcasted_iota(jnp.int32, req.shape, 0)
    halo_slot = lax.broadcasted_iota(jnp.int32, halo.shape, 0)
    req = jnp.where(req_slot < req_count_ref[...], req, -1)
    halo = jnp.where(halo_slot < halo_count_ref[...], halo, -1)
    rest = jnp.full((LANES - req.shape[0] - halo.shape[0], req.shape[1]), -1, jnp.int32)
    out_ref[...] = jnp.concatenate([req, halo, rest], axis=0).T


def pack_ids(req_t, halo_t, req_count, halo_count):
    owners = req_t.shape[1]
    return pl.pallas_call(
        pack_kernel,
        out_specs=pl.BlockSpec(memory_space=pltpu.VMEM),
        out_shape=pltpu.VMEM((owners, LANES), jnp.int32),
        name="pack_ids",
    )(req_t, halo_t, req_count, halo_count)


def project_kernel(
    features_ref, history_ref, w_in_ref, proj_ref, hist_ref,
    rows_ref, old_ref, w_ref, row_sem, old_sem, w_sem,
):
    step = PROJECT_STEP
    steps = proj_ref.shape[0] // step

    def fetch(k):
        at = pl.ds(k * step, step)
        return pltpu.make_async_copy(features_ref.at[at], rows_ref.at[at], row_sem.at[k])

    old = pltpu.make_async_copy(history_ref, old_ref, old_sem)
    weights = pltpu.make_async_copy(w_in_ref, w_ref, w_sem)
    old.start()
    weights.start()
    for k in range(steps):
        fetch(k).start()
    old.wait()
    hist_ref[...] = old_ref[...].astype(jnp.bfloat16)
    weights.wait()

    @pl.loop(0, steps)
    def _(k):
        fetch(k).wait()
        at = pl.ds(pl.multiple_of(k * step, step), step)
        proj_ref[at] = jnp.dot(
            rows_ref[at].astype(jnp.bfloat16), w_ref[...], preferred_element_type=jnp.float32
        ).astype(jnp.bfloat16)


def project(features, history, w_in):
    rows, width = features.shape
    hidden = w_in.shape[1]
    table = pltpu.VMEM((rows, hidden), jnp.bfloat16)
    features = pltpu.with_memory_space_constraint(features, pltpu.HBM)
    history = pltpu.with_memory_space_constraint(history, pltpu.HBM)
    w_in = pltpu.with_memory_space_constraint(w_in, pltpu.HBM)
    vmem = pl.BlockSpec(memory_space=pltpu.VMEM)
    hbm = pl.BlockSpec(memory_space=pltpu.HBM)
    return pl.pallas_call(
        project_kernel,
        in_specs=[hbm, hbm, hbm],
        out_specs=[vmem, vmem],
        out_shape=[table, table],
        scratch_shapes=[
            pltpu.VMEM((rows, width), jnp.float32),
            pltpu.VMEM((rows, hidden), jnp.float32),
            pltpu.VMEM((width, hidden), jnp.bfloat16),
            pltpu.SemaphoreType.DMA((rows // PROJECT_STEP,)),
            pltpu.SemaphoreType.DMA,
            pltpu.SemaphoreType.DMA,
        ],
        cost_estimate=pl.CostEstimate(
            flops=2 * rows * width * hidden, bytes_accessed=5 << 20, transcendentals=0
        ),
        compiler_params=pltpu.CompilerParams(vmem_limit_bytes=60 << 20),
        name="project",
    )(features, history, w_in)


def pick_kernel(req, halo, ids_ref, proj_ref, hist_ref, out_ref, req_ref, halo_ref, sem):
    count = ids_ref.shape[0]
    rows = proj_ref.shape[0]
    turned = ids_ref[...].T

    def pick(table_ref, start, size, first, last):
        wide = jnp.concatenate(
            [
                jnp.broadcast_to(turned[start : start + size, c : c + 1], (size, LANES))
                for c in range(first, last)
            ],
            axis=0,
        )
        high = (wide >> 7).astype(jnp.float32).astype(jnp.bfloat16)
        low = (wide & (LANES - 1)).astype(jnp.float32).astype(jnp.bfloat16)
        lane = lax.broadcasted_iota(jnp.int32, wide.shape, 1)
        lane = lane.astype(jnp.float32).astype(jnp.bfloat16)
        one, zero = jnp.ones_like(low), jnp.zeros_like(low)
        hit = jnp.where(low == lane, one, zero)
        parts = [
            jnp.where(high == jnp.full_like(high, k), hit, zero) for k in range(rows // LANES)
        ]
        picked = jnp.dot(
            jnp.concatenate(parts, axis=1), table_ref[...], preferred_element_type=jnp.float32
        )
        return picked.astype(jnp.bfloat16).reshape(last - first, size, -1)

    copies = []

    def send(held_ref, start, size, first, last):
        copy = pltpu.make_async_copy(
            held_ref.at[first:last],
            out_ref.at[first:last, start : start + size, :],
            sem.at[len(copies)],
        )
        copy.start()
        copies.append(copy)

    halo_ref[...] = pick(hist_ref, req, halo, 0, count)
    send(halo_ref, req, halo, 0, count)
    part = count // PICK_PARTS
    for first in range(0, count, part):
        req_ref[first : first + part] = pick(proj_ref, 0, req, first, first + part)
        send(req_ref, 0, req, first, first + part)
    for copy in copies:
        copy.wait()


def pick_rows(ids, proj, hist, req, halo):
    count = ids.shape[0]
    hidden = proj.shape[1]
    flops = 2 * count * (req + halo) * proj.shape[0] * hidden
    vmem = pl.BlockSpec(memory_space=pltpu.VMEM)
    return pl.pallas_call(
        functools.partial(pick_kernel, req, halo),
        in_specs=[vmem, vmem, vmem],
        out_specs=pl.BlockSpec(memory_space=pltpu.HBM),
        out_shape=jax.ShapeDtypeStruct((count, req + halo, hidden), jnp.bfloat16),
        scratch_shapes=[
            pltpu.VMEM((count, req, hidden), jnp.bfloat16),
            pltpu.VMEM((count, halo, hidden), jnp.bfloat16),
            pltpu.SemaphoreType.DMA((1 + PICK_PARTS,)),
        ],
        cost_estimate=pl.CostEstimate(flops=flops, bytes_accessed=3 << 20, transcendentals=0),
        compiler_params=pltpu.CompilerParams(vmem_limit_bytes=24 << 20),
        name="pick_rows",
    )(ids, proj, hist)


def dense_kernel(
    rows_ref, cols_ref, used_ref, tiles_ref, kept_ref, out_ref,
    held_ref, acc_ref, stage_ref, in_sem, out_sem,
):
    slots, side, _ = tiles_ref.shape
    blocks = acc_ref.shape[0] - 1
    kept_blocks = kept_ref.shape[0] // side
    row_blocks, width = out_ref.shape[0] // side, out_ref.shape[1]
    col_blocks = width // side
    chunk = slots // TILE_CHUNKS

    def fetch(c):
        at = pl.ds(c * chunk, chunk)
        return pltpu.make_async_copy(tiles_ref.at[at], held_ref.at[at], in_sem.at[c])

    def flush(r, slot):
        return pltpu.make_async_copy(
            stage_ref.at[slot], out_ref.at[pl.ds(r * side, side)], out_sem.at[slot]
        )

    for c in range(TILE_CHUNKS):
        fetch(c).start()

    @pl.loop(0, blocks)
    def _(b):
        acc_ref[b] = jnp.zeros(acc_ref.shape[1:], jnp.float32)

    @pl.loop(0, TILE_CHUNKS)
    def _(c):
        fetch(c).wait()

        live = jnp.clip(used_ref[0] - c * chunk, 0, chunk)

        @pl.loop(0, (live + TILE_UNROLL - 1) // TILE_UNROLL)
        def _(g):
            for u in range(TILE_UNROLL):
                t = c * chunk + g * TILE_UNROLL + u
                block = rows_ref[t] * col_blocks + cols_ref[t]
                block = jnp.where(t < used_ref[0], block, blocks)
                acc_ref[block] = acc_ref[block] + held_ref[t].astype(jnp.float32)

    @pl.loop(0, row_blocks)
    def _(r):
        slot = lax.rem(r, OUT_SLOTS)

        @pl.when(r >= OUT_SLOTS)
        def _():
            flush(r - OUT_SLOTS, slot).wait()

        for k in range(col_blocks):
            stage_ref[slot, :, k * side : (k + 1) * side] = acc_ref[
                (kept_blocks + r) * col_blocks + k
            ].astype(jnp.bfloat16)
        flush(r, slot).start()

    @pl.loop(0, kept_blocks)
    def _(r):
        at = pl.ds(pl.multiple_of(r * side, side), side)
        for k in range(col_blocks):
            kept_ref[at, k * side : (k + 1) * side] = acc_ref[r * col_blocks + k].astype(
                jnp.bfloat16
            )

    for r in range(row_blocks - OUT_SLOTS, row_blocks):
        flush(r, r % OUT_SLOTS).wait()


def build_dense(tile_rows, tile_cols, tile_count, tile_values, row_blocks, col_blocks):
    slots, side, _ = tile_values.shape
    width = col_blocks * side
    tile_values = pltpu.with_memory_space_constraint(tile_values, pltpu.HBM)
    smem = pl.BlockSpec(memory_space=pltpu.SMEM)
    hbm = pl.BlockSpec(memory_space=pltpu.HBM)
    return pl.pallas_call(
        dense_kernel,
        in_specs=[smem, smem, smem, hbm],
        out_specs=[pl.BlockSpec(memory_space=pltpu.VMEM), hbm],
        out_shape=[
            pltpu.VMEM((KEPT_ROWS, width), jnp.bfloat16),
            jax.ShapeDtypeStruct((row_blocks * side - KEPT_ROWS, width), jnp.bfloat16),
        ],
        scratch_shapes=[
            pltpu.VMEM((slots, side, side), jnp.bfloat16),
            pltpu.VMEM((row_blocks * col_blocks + 1, side, side), jnp.float32),
            pltpu.VMEM((OUT_SLOTS, side, col_blocks * side), jnp.bfloat16),
            pltpu.SemaphoreType.DMA((TILE_CHUNKS,)),
            pltpu.SemaphoreType.DMA((OUT_SLOTS,)),
        ],
        compiler_params=pltpu.CompilerParams(vmem_limit_bytes=56 << 20),
        cost_estimate=pl.CostEstimate(flops=1 << 20, bytes_accessed=30 << 20, transcendentals=0),
        name="build_dense",
    )(tile_rows, tile_cols, tile_count, tile_values)


def combine_kernel(
    req, kept_ref, dense_ref, came_ref, w_ref, out_ref,
    held_ref, source_ref, stage_ref, kept_sem, in_sem, out_sem,
):
    owners, slots, hidden = came_ref.shape
    nodes = owners * req
    step = ROWS_STEP
    steps = nodes // step

    kept = kept_ref.shape[0]

    def fetch(first, size, k):
        return pltpu.make_async_copy(
            dense_ref.at[pl.ds(first - kept, size)], held_ref.at[pl.ds(first, size)], in_sem.at[k]
        )

    def fetch_step(k):
        return fetch(k * step, step, k)

    near = pltpu.make_async_copy(kept_ref, held_ref.at[pl.ds(0, kept)], kept_sem)
    start = fetch(kept, step - kept, 0)

    def flush(k):
        at = pl.ds(k * step, step)
        return pltpu.make_async_copy(stage_ref.at[at], out_ref.at[at], out_sem.at[k])

    start.start()
    near.start()
    fetch_step(1).start()
    source_ref[:nodes] = came_ref[:, :req, :].reshape(nodes, hidden)
    source_ref[nodes:] = came_ref[:, req:, :].reshape(owners * (slots - req), hidden)

    @pl.loop(0, steps)
    def _(k):
        @pl.when(k == 0)
        def _():
            start.wait()
            near.wait()

        @pl.when(k > 0)
        def _():
            fetch_step(k).wait()

        @pl.when(k + 2 < steps)
        def _():
            fetch_step(k + 2).start()

        at = pl.ds(pl.multiple_of(k * step, step), step)
        total = jnp.dot(held_ref[at], source_ref[...], preferred_element_type=jnp.float32)
        mixed = jnp.dot(total.astype(jnp.bfloat16), w_ref[...], preferred_element_type=jnp.float32)
        own = source_ref[at].astype(jnp.float32)
        stage_ref[at] = jnp.maximum(mixed + own, 0.0).astype(jnp.bfloat16)
        flush(k).start()

    for k in range(steps):
        flush(k).wait()


def combine(kept, dense, came, w_out, req):
    hidden = came.shape[2]
    nodes, width = kept.shape[0] + dense.shape[0], dense.shape[1]
    dense = pltpu.with_memory_space_constraint(dense, pltpu.HBM)
    vmem = pl.BlockSpec(memory_space=pltpu.VMEM)
    hbm = pl.BlockSpec(memory_space=pltpu.HBM)
    return pl.pallas_call(
        functools.partial(combine_kernel, req),
        in_specs=[vmem, hbm, vmem, vmem],
        out_specs=hbm,
        out_shape=jax.ShapeDtypeStruct((nodes, hidden), jnp.bfloat16),
        scratch_shapes=[
            pltpu.VMEM((nodes, width), jnp.bfloat16),
            pltpu.VMEM((width, hidden), jnp.bfloat16),
            pltpu.VMEM((nodes, hidden), jnp.bfloat16),
            pltpu.SemaphoreType.DMA,
            pltpu.SemaphoreType.DMA((nodes // ROWS_STEP,)),
            pltpu.SemaphoreType.DMA((nodes // ROWS_STEP,)),
        ],
        cost_estimate=pl.CostEstimate(
            flops=2 * nodes * width * hidden, bytes_accessed=16 << 20, transcendentals=0
        ),
        compiler_params=pltpu.CompilerParams(vmem_limit_bytes=24 << 20),
        name="combine",
    )(kept, dense, came, w_out)


def on_device(
    features,
    history,
    request_ids,
    request_count,
    halo_ids,
    halo_count,
    tile_values,
    tile_rows,
    tile_cols,
    tile_count,
    w_in,
    w_out,
):
    owners, req = request_ids.shape[1:]
    halo = halo_ids.shape[2]
    side = tile_values.shape[1]
    wanted = pack_ids(request_ids[0].T, halo_ids[0].T, request_count, halo_count)
    asked = lax.all_to_all(wanted, "nodes", split_axis=0, concat_axis=0, tiled=True)
    proj, hist = project(features, history, w_in)
    picked = pick_rows(asked, proj, hist, req, halo)
    picked, tile_count = lax.optimization_barrier((picked, tile_count))
    came = lax.all_to_all(picked, "nodes", split_axis=0, concat_axis=0, tiled=True)
    kept, dense = build_dense(
        tile_rows, tile_cols, tile_count, tile_values,
        owners * req // side, owners * (req + halo) // side,
    )
    return combine(kept, dense, came, w_out, req)


def solution(mesh):
    in_specs = (
        P("nodes", None),
        P("nodes", None),
        P("nodes", None, None),
        P("nodes", None),
        P("nodes", None, None),
        P("nodes", None),
        P("nodes", None, None),
        P("nodes"),
        P("nodes"),
        P("nodes"),
        P(),
        P(),
    )
    out_specs = P("nodes", None)
    return jax.shard_map(
        on_device, mesh=mesh, in_specs=in_specs, out_specs=out_specs, check_vma=False
    )
```

```python
import functools

import jax
import jax.numpy as jnp
from jax import lax
from jax.experimental import pallas as pl
from jax.experimental.pallas import tpu as pltpu
from jax.sharding import PartitionSpec as P

LANES = 128
TILE_CHUNKS = 8
TILE_UNROLL = 4
OUT_SLOTS = 8
PICK_CUTS = (0, 2, 4, 6, 7, 8)
ROWS_STEP = 512
KEPT_ROWS = 256
PROJECT_STEP = 512


def pack_kernel(req_ref, halo_ref, req_count_ref, halo_count_ref, out_ref):
    req = req_ref[...]
    halo = halo_ref[...]
    req_slot = lax.broadcasted_iota(jnp.int32, req.shape, 0)
    halo_slot = lax.broadcasted_iota(jnp.int32, halo.shape, 0)
    req = jnp.where(req_slot < req_count_ref[...], req, -1)
    halo = jnp.where(halo_slot < halo_count_ref[...], halo, -1)
    rest = jnp.full((LANES - req.shape[0] - halo.shape[0], req.shape[1]), -1, jnp.int32)
    out_ref[...] = jnp.concatenate([req, halo, rest], axis=0).T


def pack_ids(req_t, halo_t, req_count, halo_count):
    owners = req_t.shape[1]
    return pl.pallas_call(
        pack_kernel,
        out_specs=pl.BlockSpec(memory_space=pltpu.VMEM),
        out_shape=pltpu.VMEM((owners, LANES), jnp.int32),
        name="pack_ids",
    )(req_t, halo_t, req_count, halo_count)


def project_kernel(
    features_ref, history_ref, w_in_ref, proj_ref, hist_ref,
    rows_ref, old_ref, w_ref, row_sem, old_sem, w_sem,
):
    step = PROJECT_STEP
    steps = proj_ref.shape[0] // step

    def fetch(k):
        at = pl.ds(k * step, step)
        return pltpu.make_async_copy(features_ref.at[at], rows_ref.at[at], row_sem.at[k])

    old = pltpu.make_async_copy(history_ref, old_ref, old_sem)
    weights = pltpu.make_async_copy(w_in_ref, w_ref, w_sem)
    old.start()
    weights.start()
    for k in range(steps):
        fetch(k).start()
    old.wait()
    hist_ref[...] = old_ref[...].astype(jnp.bfloat16)
    weights.wait()

    @pl.loop(0, steps)
    def _(k):
        fetch(k).wait()
        at = pl.ds(pl.multiple_of(k * step, step), step)
        proj_ref[at] = jnp.dot(
            rows_ref[at].astype(jnp.bfloat16), w_ref[...], preferred_element_type=jnp.float32
        ).astype(jnp.bfloat16)


def project(features, history, w_in):
    rows, width = features.shape
    hidden = w_in.shape[1]
    table = pltpu.VMEM((rows, hidden), jnp.bfloat16)
    features = pltpu.with_memory_space_constraint(features, pltpu.HBM)
    history = pltpu.with_memory_space_constraint(history, pltpu.HBM)
    w_in = pltpu.with_memory_space_constraint(w_in, pltpu.HBM)
    vmem = pl.BlockSpec(memory_space=pltpu.VMEM)
    hbm = pl.BlockSpec(memory_space=pltpu.HBM)
    return pl.pallas_call(
        project_kernel,
        in_specs=[hbm, hbm, hbm],
        out_specs=[vmem, vmem],
        out_shape=[table, table],
        scratch_shapes=[
            pltpu.VMEM((rows, width), jnp.float32),
            pltpu.VMEM((rows, hidden), jnp.float32),
            pltpu.VMEM((width, hidden), jnp.bfloat16),
            pltpu.SemaphoreType.DMA((rows // PROJECT_STEP,)),
            pltpu.SemaphoreType.DMA,
            pltpu.SemaphoreType.DMA,
        ],
        cost_estimate=pl.CostEstimate(
            flops=2 * rows * width * hidden, bytes_accessed=5 << 20, transcendentals=0
        ),
        compiler_params=pltpu.CompilerParams(vmem_limit_bytes=60 << 20),
        name="project",
    )(features, history, w_in)


def pick_kernel(req, halo, ids_ref, proj_ref, hist_ref, out_ref, held_ref, sem):
    count = ids_ref.shape[0]
    rows = proj_ref.shape[0]
    turned = ids_ref[...].T

    def pick(table_ref, start, size, first, last):
        wide = jnp.concatenate(
            [
                jnp.broadcast_to(turned[start : start + size, c : c + 1], (size, LANES))
                for c in range(first, last)
            ],
            axis=0,
        )
        high = (wide >> 7).astype(jnp.float32).astype(jnp.bfloat16)
        low = (wide & (LANES - 1)).astype(jnp.float32).astype(jnp.bfloat16)
        lane = lax.broadcasted_iota(jnp.int32, wide.shape, 1)
        lane = lane.astype(jnp.float32).astype(jnp.bfloat16)
        one, zero = jnp.ones_like(low), jnp.zeros_like(low)
        hit = jnp.where(low == lane, one, zero)
        parts = [
            jnp.where(high == jnp.full_like(high, k), hit, zero) for k in range(rows // LANES)
        ]
        picked = jnp.dot(
            jnp.concatenate(parts, axis=1), table_ref[...], preferred_element_type=jnp.float32
        )
        return picked.astype(jnp.bfloat16).reshape(last - first, size, -1)

    def send(first, last, k):
        at = pl.ds(first, last - first)
        return pltpu.make_async_copy(held_ref.at[at], out_ref.at[at], sem.at[k])

    cuts = [count * part // 8 for part in PICK_CUTS]
    copies = []
    for k, (first, last) in enumerate(zip(cuts[:-1], cuts[1:])):
        held_ref[first:last, :req, :] = pick(proj_ref, 0, req, first, last)
        held_ref[first:last, req:, :] = pick(hist_ref, req, halo, first, last)
        copy = send(first, last, k)
        copy.start()
        copies.append(copy)
    for copy in copies:
        copy.wait()


def pick_rows(ids, proj, hist, req, halo):
    count = ids.shape[0]
    hidden = proj.shape[1]
    flops = 2 * count * (req + halo) * proj.shape[0] * hidden
    vmem = pl.BlockSpec(memory_space=pltpu.VMEM)
    return pl.pallas_call(
        functools.partial(pick_kernel, req, halo),
        in_specs=[vmem, vmem, vmem],
        out_specs=pl.BlockSpec(memory_space=pltpu.HBM),
        out_shape=jax.ShapeDtypeStruct((count, req + halo, hidden), jnp.bfloat16),
        scratch_shapes=[
            pltpu.VMEM((count, req + halo, hidden), jnp.bfloat16),
            pltpu.SemaphoreType.DMA((len(PICK_CUTS) - 1,)),
        ],
        cost_estimate=pl.CostEstimate(flops=flops, bytes_accessed=3 << 20, transcendentals=0),
        compiler_params=pltpu.CompilerParams(vmem_limit_bytes=24 << 20),
        name="pick_rows",
    )(ids, proj, hist)


def dense_kernel(
    rows_ref, cols_ref, used_ref, tiles_ref, kept_ref, out_ref,
    held_ref, acc_ref, stage_ref, in_sem, out_sem,
):
    slots, side, _ = tiles_ref.shape
    blocks = acc_ref.shape[0] - 1
    kept_blocks = kept_ref.shape[0] // side
    row_blocks, width = out_ref.shape[0] // side, out_ref.shape[1]
    col_blocks = width // side
    chunk = slots // TILE_CHUNKS

    def fetch(c):
        at = pl.ds(c * chunk, chunk)
        return pltpu.make_async_copy(tiles_ref.at[at], held_ref.at[at], in_sem.at[c])

    def flush(r, slot):
        return pltpu.make_async_copy(
            stage_ref.at[slot], out_ref.at[pl.ds(r * side, side)], out_sem.at[slot]
        )

    for c in range(TILE_CHUNKS):
        fetch(c).start()

    @pl.loop(0, blocks)
    def _(b):
        acc_ref[b] = jnp.zeros(acc_ref.shape[1:], jnp.float32)

    @pl.loop(0, TILE_CHUNKS)
    def _(c):
        fetch(c).wait()

        live = jnp.clip(used_ref[0] - c * chunk, 0, chunk)

        @pl.loop(0, (live + TILE_UNROLL - 1) // TILE_UNROLL)
        def _(g):
            for u in range(TILE_UNROLL):
                t = c * chunk + g * TILE_UNROLL + u
                block = rows_ref[t] * col_blocks + cols_ref[t]
                block = jnp.where(t < used_ref[0], block, blocks)
                acc_ref[block] = acc_ref[block] + held_ref[t].astype(jnp.float32)

    @pl.loop(0, row_blocks)
    def _(r):
        slot = lax.rem(r, OUT_SLOTS)

        @pl.when(r >= OUT_SLOTS)
        def _():
            flush(r - OUT_SLOTS, slot).wait()

        for k in range(col_blocks):
            stage_ref[slot, :, k * side : (k + 1) * side] = acc_ref[
                (kept_blocks + r) * col_blocks + k
            ].astype(jnp.bfloat16)
        flush(r, slot).start()

    @pl.loop(0, kept_blocks)
    def _(r):
        at = pl.ds(pl.multiple_of(r * side, side), side)
        for k in range(col_blocks):
            kept_ref[at, k * side : (k + 1) * side] = acc_ref[r * col_blocks + k].astype(
                jnp.bfloat16
            )

    for r in range(row_blocks - OUT_SLOTS, row_blocks):
        flush(r, r % OUT_SLOTS).wait()


def build_dense(tile_rows, tile_cols, tile_count, tile_values, row_blocks, col_blocks):
    slots, side, _ = tile_values.shape
    width = col_blocks * side
    tile_values = pltpu.with_memory_space_constraint(tile_values, pltpu.HBM)
    smem = pl.BlockSpec(memory_space=pltpu.SMEM)
    hbm = pl.BlockSpec(memory_space=pltpu.HBM)
    return pl.pallas_call(
        dense_kernel,
        in_specs=[smem, smem, smem, hbm],
        out_specs=[pl.BlockSpec(memory_space=pltpu.VMEM), hbm],
        out_shape=[
            pltpu.VMEM((KEPT_ROWS, width), jnp.bfloat16),
            jax.ShapeDtypeStruct((row_blocks * side - KEPT_ROWS, width), jnp.bfloat16),
        ],
        scratch_shapes=[
            pltpu.VMEM((slots, side, side), jnp.bfloat16),
            pltpu.VMEM((row_blocks * col_blocks + 1, side, side), jnp.float32),
            pltpu.VMEM((OUT_SLOTS, side, col_blocks * side), jnp.bfloat16),
            pltpu.SemaphoreType.DMA((TILE_CHUNKS,)),
            pltpu.SemaphoreType.DMA((OUT_SLOTS,)),
        ],
        compiler_params=pltpu.CompilerParams(vmem_limit_bytes=56 << 20),
        cost_estimate=pl.CostEstimate(flops=1 << 20, bytes_accessed=30 << 20, transcendentals=0),
        name="build_dense",
    )(tile_rows, tile_cols, tile_count, tile_values)


def combine_kernel(
    req, kept_ref, dense_ref, came_ref, w_ref, out_ref,
    held_ref, source_ref, stage_ref, kept_sem, in_sem, out_sem,
):
    owners, slots, hidden = came_ref.shape
    nodes = owners * req
    step = ROWS_STEP
    steps = nodes // step

    kept = kept_ref.shape[0]

    def fetch(first, size, k):
        return pltpu.make_async_copy(
            dense_ref.at[pl.ds(first - kept, size)], held_ref.at[pl.ds(first, size)], in_sem.at[k]
        )

    def fetch_step(k):
        return fetch(k * step, step, k)

    near = pltpu.make_async_copy(kept_ref, held_ref.at[pl.ds(0, kept)], kept_sem)
    start = fetch(kept, step - kept, 0)

    def flush(k):
        at = pl.ds(k * step, step)
        return pltpu.make_async_copy(stage_ref.at[at], out_ref.at[at], out_sem.at[k])

    start.start()
    near.start()
    fetch_step(1).start()
    source_ref[:nodes] = came_ref[:, :req, :].reshape(nodes, hidden)
    source_ref[nodes:] = came_ref[:, req:, :].reshape(owners * (slots - req), hidden)

    @pl.loop(0, steps)
    def _(k):
        @pl.when(k == 0)
        def _():
            start.wait()
            near.wait()

        @pl.when(k > 0)
        def _():
            fetch_step(k).wait()

        @pl.when(k + 2 < steps)
        def _():
            fetch_step(k + 2).start()

        at = pl.ds(pl.multiple_of(k * step, step), step)
        total = jnp.dot(held_ref[at], source_ref[...], preferred_element_type=jnp.float32)
        mixed = jnp.dot(total.astype(jnp.bfloat16), w_ref[...], preferred_element_type=jnp.float32)
        own = source_ref[at].astype(jnp.float32)
        stage_ref[at] = jnp.maximum(mixed + own, 0.0).astype(jnp.bfloat16)
        flush(k).start()

    for k in range(steps):
        flush(k).wait()


def combine(kept, dense, came, w_out, req):
    hidden = came.shape[2]
    nodes, width = kept.shape[0] + dense.shape[0], dense.shape[1]
    dense = pltpu.with_memory_space_constraint(dense, pltpu.HBM)
    vmem = pl.BlockSpec(memory_space=pltpu.VMEM)
    hbm = pl.BlockSpec(memory_space=pltpu.HBM)
    return pl.pallas_call(
        functools.partial(combine_kernel, req),
        in_specs=[vmem, hbm, vmem, vmem],
        out_specs=hbm,
        out_shape=jax.ShapeDtypeStruct((nodes, hidden), jnp.bfloat16),
        scratch_shapes=[
            pltpu.VMEM((nodes, width), jnp.bfloat16),
            pltpu.VMEM((width, hidden), jnp.bfloat16),
            pltpu.VMEM((nodes, hidden), jnp.bfloat16),
            pltpu.SemaphoreType.DMA,
            pltpu.SemaphoreType.DMA((nodes // ROWS_STEP,)),
            pltpu.SemaphoreType.DMA((nodes // ROWS_STEP,)),
        ],
        cost_estimate=pl.CostEstimate(
            flops=2 * nodes * width * hidden, bytes_accessed=16 << 20, transcendentals=0
        ),
        compiler_params=pltpu.CompilerParams(vmem_limit_bytes=24 << 20),
        name="combine",
    )(kept, dense, came, w_out)


def on_device(
    features,
    history,
    request_ids,
    request_count,
    halo_ids,
    halo_count,
    tile_values,
    tile_rows,
    tile_cols,
    tile_count,
    w_in,
    w_out,
):
    owners, req = request_ids.shape[1:]
    halo = halo_ids.shape[2]
    side = tile_values.shape[1]
    wanted = pack_ids(request_ids[0].T, halo_ids[0].T, request_count, halo_count)
    asked = lax.all_to_all(wanted, "nodes", split_axis=0, concat_axis=0, tiled=True)
    proj, hist = project(features, history, w_in)
    picked = pick_rows(asked, proj, hist, req, halo)
    picked, tile_count = lax.optimization_barrier((picked, tile_count))
    came = lax.all_to_all(picked, "nodes", split_axis=0, concat_axis=0, tiled=True)
    kept, dense = build_dense(
        tile_rows, tile_cols, tile_count, tile_values,
        owners * req // side, owners * (req + halo) // side,
    )
    return combine(kept, dense, came, w_out, req)


def solution(mesh):
    in_specs = (
        P("nodes", None),
        P("nodes", None),
        P("nodes", None, None),
        P("nodes", None),
        P("nodes", None, None),
        P("nodes", None),
        P("nodes", None, None),
        P("nodes"),
        P("nodes"),
        P("nodes"),
        P(),
        P(),
    )
    out_specs = P("nodes", None)
    return jax.shard_map(
        on_device, mesh=mesh, in_specs=in_specs, out_specs=out_specs, check_vma=False
    )
```

```python
import functools

import jax
import jax.numpy as jnp
from jax import lax
from jax.experimental import pallas as pl
from jax.experimental.pallas import tpu as pltpu
from jax.sharding import PartitionSpec as P

LANES = 128
TILE_CHUNKS = 8
TILE_UNROLL = 4
OUT_SLOTS = 8
PICK_CUTS = (0, 2, 4, 6, 7, 8)
ROWS_STEP = 512
KEPT_ROWS = 256
PROJECT_STEP = 512


def pack_kernel(req_ref, halo_ref, req_count_ref, halo_count_ref, out_ref):
    req = req_ref[...]
    halo = halo_ref[...]
    req_slot = lax.broadcasted_iota(jnp.int32, req.shape, 0)
    halo_slot = lax.broadcasted_iota(jnp.int32, halo.shape, 0)
    req = jnp.where(req_slot < req_count_ref[...], req, -1)
    halo = jnp.where(halo_slot < halo_count_ref[...], halo, -1)
    rest = jnp.full((LANES - req.shape[0] - halo.shape[0], req.shape[1]), -1, jnp.int32)
    out_ref[...] = jnp.concatenate([req, halo, rest], axis=0).T


def pack_ids(req_t, halo_t, req_count, halo_count):
    owners = req_t.shape[1]
    return pl.pallas_call(
        pack_kernel,
        out_specs=pl.BlockSpec(memory_space=pltpu.VMEM),
        out_shape=pltpu.VMEM((owners, LANES), jnp.int32),
        name="pack_ids",
    )(req_t, halo_t, req_count, halo_count)


def project_kernel(
    features_ref, history_ref, w_in_ref, proj_ref, hist_ref,
    rows_ref, old_ref, w_ref, row_sem, old_sem, w_sem,
):
    step = PROJECT_STEP
    steps = proj_ref.shape[0] // step

    def fetch(k):
        at = pl.ds(k * step, step)
        return pltpu.make_async_copy(features_ref.at[at], rows_ref.at[at], row_sem.at[k])

    old = pltpu.make_async_copy(history_ref, old_ref, old_sem)
    weights = pltpu.make_async_copy(w_in_ref, w_ref, w_sem)
    old.start()
    weights.start()
    for k in range(steps):
        fetch(k).start()
    old.wait()
    hist_ref[...] = old_ref[...].astype(jnp.bfloat16)
    weights.wait()

    @pl.loop(0, steps)
    def _(k):
        fetch(k).wait()
        at = pl.ds(pl.multiple_of(k * step, step), step)
        proj_ref[at] = jnp.dot(
            rows_ref[at].astype(jnp.bfloat16), w_ref[...], preferred_element_type=jnp.float32
        ).astype(jnp.bfloat16)


def project(features, history, w_in):
    rows, width = features.shape
    hidden = w_in.shape[1]
    table = pltpu.VMEM((rows, hidden), jnp.bfloat16)
    features = pltpu.with_memory_space_constraint(features, pltpu.HBM)
    history = pltpu.with_memory_space_constraint(history, pltpu.HBM)
    w_in = pltpu.with_memory_space_constraint(w_in, pltpu.HBM)
    vmem = pl.BlockSpec(memory_space=pltpu.VMEM)
    hbm = pl.BlockSpec(memory_space=pltpu.HBM)
    return pl.pallas_call(
        project_kernel,
        in_specs=[hbm, hbm, hbm],
        out_specs=[vmem, vmem],
        out_shape=[table, table],
        scratch_shapes=[
            pltpu.VMEM((rows, width), jnp.float32),
            pltpu.VMEM((rows, hidden), jnp.float32),
            pltpu.VMEM((width, hidden), jnp.bfloat16),
            pltpu.SemaphoreType.DMA((rows // PROJECT_STEP,)),
            pltpu.SemaphoreType.DMA,
            pltpu.SemaphoreType.DMA,
        ],
        cost_estimate=pl.CostEstimate(
            flops=2 * rows * width * hidden, bytes_accessed=5 << 20, transcendentals=0
        ),
        compiler_params=pltpu.CompilerParams(vmem_limit_bytes=60 << 20),
        name="project",
    )(features, history, w_in)


def pick_kernel(req, halo, ids_ref, proj_ref, hist_ref, out_ref, held_ref, sem):
    count = ids_ref.shape[0]
    rows = proj_ref.shape[0]
    turned = ids_ref[...].T

    def pick(table_ref, start, size, first, last):
        wide = jnp.concatenate(
            [
                jnp.broadcast_to(turned[start : start + size, c : c + 1], (size, LANES))
                for c in range(first, last)
            ],
            axis=0,
        )
        high = (wide >> 7).astype(jnp.float32).astype(jnp.bfloat16)
        low = (wide & (LANES - 1)).astype(jnp.float32).astype(jnp.bfloat16)
        lane = lax.broadcasted_iota(jnp.int32, wide.shape, 1)
        lane = lane.astype(jnp.float32).astype(jnp.bfloat16)
        one, zero = jnp.ones_like(low), jnp.zeros_like(low)
        hit = jnp.where(low == lane, one, zero)
        parts = [
            jnp.where(high == jnp.full_like(high, k), hit, zero) for k in range(rows // LANES)
        ]
        picked = jnp.dot(
            jnp.concatenate(parts, axis=1), table_ref[...], preferred_element_type=jnp.float32
        )
        return picked.astype(jnp.bfloat16).reshape(last - first, size, -1)

    def send(first, last, k):
        at = pl.ds(first, last - first)
        return pltpu.make_async_copy(held_ref.at[at], out_ref.at[at], sem.at[k])

    cuts = [count * part // 8 for part in PICK_CUTS]
    copies = []
    for k, (first, last) in enumerate(zip(cuts[:-1], cuts[1:])):
        held_ref[first:last, :req, :] = pick(proj_ref, 0, req, first, last)
        held_ref[first:last, req:, :] = pick(hist_ref, req, halo, first, last)
        copy = send(first, last, k)
        copy.start()
        copies.append(copy)
    for copy in copies:
        copy.wait()


def pick_rows(ids, proj, hist, req, halo):
    count = ids.shape[0]
    hidden = proj.shape[1]
    flops = 2 * count * (req + halo) * proj.shape[0] * hidden
    vmem = pl.BlockSpec(memory_space=pltpu.VMEM)
    return pl.pallas_call(
        functools.partial(pick_kernel, req, halo),
        in_specs=[vmem, vmem, vmem],
        out_specs=pl.BlockSpec(memory_space=pltpu.HBM),
        out_shape=jax.ShapeDtypeStruct((count, req + halo, hidden), jnp.bfloat16),
        scratch_shapes=[
            pltpu.VMEM((count, req + halo, hidden), jnp.bfloat16),
            pltpu.SemaphoreType.DMA((len(PICK_CUTS) - 1,)),
        ],
        cost_estimate=pl.CostEstimate(flops=flops, bytes_accessed=3 << 20, transcendentals=0),
        compiler_params=pltpu.CompilerParams(vmem_limit_bytes=24 << 20),
        name="pick_rows",
    )(ids, proj, hist)


def dense_kernel(
    rows_ref, cols_ref, used_ref, tiles_ref, kept_ref, out_ref,
    held_ref, acc_ref, stage_ref, in_sem, out_sem,
):
    slots, side, _ = tiles_ref.shape
    blocks = acc_ref.shape[0] - 1
    kept_blocks = kept_ref.shape[0] // side
    row_blocks, width = out_ref.shape[0] // side, out_ref.shape[1]
    col_blocks = width // side
    chunk = slots // TILE_CHUNKS

    def fetch(c):
        at = pl.ds(c * chunk, chunk)
        return pltpu.make_async_copy(tiles_ref.at[at], held_ref.at[at], in_sem.at[c])

    def flush(r, slot):
        return pltpu.make_async_copy(
            stage_ref.at[slot], out_ref.at[pl.ds(r * side, side)], out_sem.at[slot]
        )

    for c in range(TILE_CHUNKS):
        fetch(c).start()

    @pl.loop(0, blocks)
    def _(b):
        acc_ref[b] = jnp.zeros(acc_ref.shape[1:], jnp.float32)

    @pl.loop(0, TILE_CHUNKS)
    def _(c):
        fetch(c).wait()

        live = jnp.clip(used_ref[0] - c * chunk, 0, chunk)

        @pl.loop(0, (live + TILE_UNROLL - 1) // TILE_UNROLL)
        def _(g):
            for u in range(TILE_UNROLL):
                t = c * chunk + g * TILE_UNROLL + u
                block = rows_ref[t] * col_blocks + cols_ref[t]
                block = jnp.where(t < used_ref[0], block, blocks)
                acc_ref[block] = acc_ref[block] + held_ref[t].astype(jnp.float32)

    @pl.loop(0, row_blocks)
    def _(r):
        slot = lax.rem(r, OUT_SLOTS)

        @pl.when(r >= OUT_SLOTS)
        def _():
            flush(r - OUT_SLOTS, slot).wait()

        for k in range(col_blocks):
            stage_ref[slot, :, k * side : (k + 1) * side] = acc_ref[
                (kept_blocks + r) * col_blocks + k
            ].astype(jnp.bfloat16)
        flush(r, slot).start()

    @pl.loop(0, kept_blocks)
    def _(r):
        at = pl.ds(pl.multiple_of(r * side, side), side)
        for k in range(col_blocks):
            kept_ref[at, k * side : (k + 1) * side] = acc_ref[r * col_blocks + k].astype(
                jnp.bfloat16
            )

    for r in range(row_blocks - OUT_SLOTS, row_blocks):
        flush(r, r % OUT_SLOTS).wait()


def build_dense(tile_rows, tile_cols, tile_count, tile_values, row_blocks, col_blocks):
    slots, side, _ = tile_values.shape
    width = col_blocks * side
    tile_values = pltpu.with_memory_space_constraint(tile_values, pltpu.HBM)
    smem = pl.BlockSpec(memory_space=pltpu.SMEM)
    hbm = pl.BlockSpec(memory_space=pltpu.HBM)
    return pl.pallas_call(
        dense_kernel,
        in_specs=[smem, smem, smem, hbm],
        out_specs=[pl.BlockSpec(memory_space=pltpu.VMEM), hbm],
        out_shape=[
            pltpu.VMEM((KEPT_ROWS, width), jnp.bfloat16),
            jax.ShapeDtypeStruct((row_blocks * side - KEPT_ROWS, width), jnp.bfloat16),
        ],
        scratch_shapes=[
            pltpu.VMEM((slots, side, side), jnp.bfloat16),
            pltpu.VMEM((row_blocks * col_blocks + 1, side, side), jnp.float32),
            pltpu.VMEM((OUT_SLOTS, side, col_blocks * side), jnp.bfloat16),
            pltpu.SemaphoreType.DMA((TILE_CHUNKS,)),
            pltpu.SemaphoreType.DMA((OUT_SLOTS,)),
        ],
        compiler_params=pltpu.CompilerParams(vmem_limit_bytes=56 << 20),
        cost_estimate=pl.CostEstimate(flops=1 << 20, bytes_accessed=30 << 20, transcendentals=0),
        name="build_dense",
    )(tile_rows, tile_cols, tile_count, tile_values)


def combine_kernel(
    req, kept_ref, dense_ref, came_ref, w_ref, out_ref,
    held_ref, source_ref, mixed_ref, stage_ref, kept_sem, in_sem, out_sem,
):
    owners, slots, hidden = came_ref.shape
    nodes = owners * req
    step = ROWS_STEP
    steps = nodes // step

    kept = kept_ref.shape[0]

    def fetch(first, size, k):
        return pltpu.make_async_copy(
            dense_ref.at[pl.ds(first - kept, size)], held_ref.at[pl.ds(first, size)], in_sem.at[k]
        )

    def fetch_step(k):
        return fetch(k * step, step, k)

    near = pltpu.make_async_copy(kept_ref, held_ref.at[pl.ds(0, kept)], kept_sem)
    start = fetch(kept, step - kept, 0)

    def flush(k):
        at = pl.ds(k * step, step)
        return pltpu.make_async_copy(stage_ref.at[at], out_ref.at[at], out_sem.at[k])

    start.start()
    near.start()
    fetch_step(1).start()
    source_ref[:nodes] = came_ref[:, :req, :].reshape(nodes, hidden)
    source_ref[nodes:] = came_ref[:, req:, :].reshape(owners * (slots - req), hidden)

    @pl.loop(0, 3)
    def _(j):
        at = pl.ds(pl.multiple_of(j * 1024, 1024), 1024)
        mixed_ref[at] = jnp.dot(
            source_ref[at], w_ref[...], preferred_element_type=jnp.float32
        ).astype(jnp.bfloat16)

    @pl.loop(0, steps)
    def _(k):
        @pl.when(k == 0)
        def _():
            start.wait()
            near.wait()

        @pl.when(k > 0)
        def _():
            fetch_step(k).wait()

        @pl.when(k + 2 < steps)
        def _():
            fetch_step(k + 2).start()

        at = pl.ds(pl.multiple_of(k * step, step), step)
        mixed = jnp.dot(held_ref[at], mixed_ref[...], preferred_element_type=jnp.float32)
        own = source_ref[at].astype(jnp.float32)
        stage_ref[at] = jnp.maximum(mixed + own, 0.0).astype(jnp.bfloat16)
        flush(k).start()

    for k in range(steps):
        flush(k).wait()


def combine(kept, dense, came, w_out, req):
    hidden = came.shape[2]
    nodes, width = kept.shape[0] + dense.shape[0], dense.shape[1]
    dense = pltpu.with_memory_space_constraint(dense, pltpu.HBM)
    vmem = pl.BlockSpec(memory_space=pltpu.VMEM)
    hbm = pl.BlockSpec(memory_space=pltpu.HBM)
    return pl.pallas_call(
        functools.partial(combine_kernel, req),
        in_specs=[vmem, hbm, vmem, vmem],
        out_specs=hbm,
        out_shape=jax.ShapeDtypeStruct((nodes, hidden), jnp.bfloat16),
        scratch_shapes=[
            pltpu.VMEM((nodes, width), jnp.bfloat16),
            pltpu.VMEM((width, hidden), jnp.bfloat16),
            pltpu.VMEM((width, hidden), jnp.bfloat16),
            pltpu.VMEM((nodes, hidden), jnp.bfloat16),
            pltpu.SemaphoreType.DMA,
            pltpu.SemaphoreType.DMA((nodes // ROWS_STEP,)),
            pltpu.SemaphoreType.DMA((nodes // ROWS_STEP,)),
        ],
        cost_estimate=pl.CostEstimate(
            flops=2 * nodes * width * hidden, bytes_accessed=16 << 20, transcendentals=0
        ),
        compiler_params=pltpu.CompilerParams(vmem_limit_bytes=24 << 20),
        name="combine",
    )(kept, dense, came, w_out)


def on_device(
    features,
    history,
    request_ids,
    request_count,
    halo_ids,
    halo_count,
    tile_values,
    tile_rows,
    tile_cols,
    tile_count,
    w_in,
    w_out,
):
    owners, req = request_ids.shape[1:]
    halo = halo_ids.shape[2]
    side = tile_values.shape[1]
    wanted = pack_ids(request_ids[0].T, halo_ids[0].T, request_count, halo_count)
    asked = lax.all_to_all(wanted, "nodes", split_axis=0, concat_axis=0, tiled=True)
    proj, hist = project(features, history, w_in)
    picked = pick_rows(asked, proj, hist, req, halo)
    picked, tile_count = lax.optimization_barrier((picked, tile_count))
    came = lax.all_to_all(picked, "nodes", split_axis=0, concat_axis=0, tiled=True)
    kept, dense = build_dense(
        tile_rows, tile_cols, tile_count, tile_values,
        owners * req // side, owners * (req + halo) // side,
    )
    return combine(kept, dense, came, w_out, req)


def solution(mesh):
    in_specs = (
        P("nodes", None),
        P("nodes", None),
        P("nodes", None, None),
        P("nodes", None),
        P("nodes", None, None),
        P("nodes", None),
        P("nodes", None, None),
        P("nodes"),
        P("nodes"),
        P("nodes"),
        P(),
        P(),
    )
    out_specs = P("nodes", None)
    return jax.shard_map(
        on_device, mesh=mesh, in_specs=in_specs, out_specs=out_specs, check_vma=False
    )
```

```python
import functools

import jax
import jax.numpy as jnp
from jax import lax
from jax.experimental import pallas as pl
from jax.experimental.pallas import tpu as pltpu
from jax.sharding import PartitionSpec as P

LANES = 128
TILE_CHUNKS = 8
TILE_UNROLL = 4
OUT_SLOTS = 8
PICK_CUTS = (0, 2, 4, 6, 7, 8)
ROWS_STEP = 512
KEPT_ROWS = 256
PROJECT_STEP = 512


def pack_kernel(req_ref, halo_ref, req_count_ref, halo_count_ref, out_ref):
    req = req_ref[...]
    halo = halo_ref[...]
    req_slot = lax.broadcasted_iota(jnp.int32, req.shape, 0)
    halo_slot = lax.broadcasted_iota(jnp.int32, halo.shape, 0)
    req = jnp.where(req_slot < req_count_ref[...], req, -1)
    halo = jnp.where(halo_slot < halo_count_ref[...], halo, -1)
    rest = jnp.full((LANES - req.shape[0] - halo.shape[0], req.shape[1]), -1, jnp.int32)
    out_ref[...] = jnp.concatenate([req, halo, rest], axis=0).T


def pack_ids(req_t, halo_t, req_count, halo_count):
    owners = req_t.shape[1]
    return pl.pallas_call(
        pack_kernel,
        out_specs=pl.BlockSpec(memory_space=pltpu.VMEM),
        out_shape=pltpu.VMEM((owners, LANES), jnp.int32),
        name="pack_ids",
    )(req_t, halo_t, req_count, halo_count)


def project_kernel(
    features_ref, history_ref, w_in_ref, proj_ref, hist_ref,
    rows_ref, old_ref, w_ref, row_sem, old_sem, w_sem,
):
    step = PROJECT_STEP
    steps = proj_ref.shape[0] // step

    def fetch(k):
        at = pl.ds(k * step, step)
        return pltpu.make_async_copy(features_ref.at[at], rows_ref.at[at], row_sem.at[k])

    old = pltpu.make_async_copy(history_ref, old_ref, old_sem)
    weights = pltpu.make_async_copy(w_in_ref, w_ref, w_sem)
    old.start()
    weights.start()
    for k in range(steps):
        fetch(k).start()
    old.wait()
    hist_ref[...] = old_ref[...].astype(jnp.bfloat16)
    weights.wait()

    @pl.loop(0, steps)
    def _(k):
        fetch(k).wait()
        at = pl.ds(pl.multiple_of(k * step, step), step)
        proj_ref[at] = jnp.dot(
            rows_ref[at].astype(jnp.bfloat16), w_ref[...], preferred_element_type=jnp.float32
        ).astype(jnp.bfloat16)


def project(features, history, w_in):
    rows, width = features.shape
    hidden = w_in.shape[1]
    table = pltpu.VMEM((rows, hidden), jnp.bfloat16)
    features = pltpu.with_memory_space_constraint(features, pltpu.HBM)
    history = pltpu.with_memory_space_constraint(history, pltpu.HBM)
    w_in = pltpu.with_memory_space_constraint(w_in, pltpu.HBM)
    vmem = pl.BlockSpec(memory_space=pltpu.VMEM)
    hbm = pl.BlockSpec(memory_space=pltpu.HBM)
    return pl.pallas_call(
        project_kernel,
        in_specs=[hbm, hbm, hbm],
        out_specs=[vmem, vmem],
        out_shape=[table, table],
        scratch_shapes=[
            pltpu.VMEM((rows, width), jnp.float32),
            pltpu.VMEM((rows, hidden), jnp.float32),
            pltpu.VMEM((width, hidden), jnp.bfloat16),
            pltpu.SemaphoreType.DMA((rows // PROJECT_STEP,)),
            pltpu.SemaphoreType.DMA,
            pltpu.SemaphoreType.DMA,
        ],
        cost_estimate=pl.CostEstimate(
            flops=2 * rows * width * hidden, bytes_accessed=5 << 20, transcendentals=0
        ),
        compiler_params=pltpu.CompilerParams(vmem_limit_bytes=60 << 20),
        name="project",
    )(features, history, w_in)


def pick_kernel(req, halo, ids_ref, proj_ref, hist_ref, out_ref, held_ref, sem):
    count = ids_ref.shape[0]
    rows = proj_ref.shape[0]
    turned = ids_ref[...].T

    def pick(table_ref, start, size, first, last):
        wide = jnp.concatenate(
            [
                jnp.broadcast_to(turned[start : start + size, c : c + 1], (size, LANES))
                for c in range(first, last)
            ],
            axis=0,
        )
        high = (wide >> 7).astype(jnp.float32).astype(jnp.bfloat16)
        low = (wide & (LANES - 1)).astype(jnp.float32).astype(jnp.bfloat16)
        lane = lax.broadcasted_iota(jnp.int32, wide.shape, 1)
        lane = lane.astype(jnp.float32).astype(jnp.bfloat16)
        one, zero = jnp.ones_like(low), jnp.zeros_like(low)
        hit = jnp.where(low == lane, one, zero)
        parts = [
            jnp.where(high == jnp.full_like(high, k), hit, zero) for k in range(rows // LANES)
        ]
        picked = jnp.dot(
            jnp.concatenate(parts, axis=1), table_ref[...], preferred_element_type=jnp.float32
        )
        return picked.astype(jnp.bfloat16).reshape(last - first, size, -1)

    def send(first, last, k):
        at = pl.ds(first, last - first)
        return pltpu.make_async_copy(held_ref.at[at], out_ref.at[at], sem.at[k])

    cuts = [count * part // 8 for part in PICK_CUTS]
    copies = []
    for k, (first, last) in enumerate(zip(cuts[:-1], cuts[1:])):
        held_ref[first:last, :req, :] = pick(proj_ref, 0, req, first, last)
        held_ref[first:last, req:, :] = pick(hist_ref, req, halo, first, last)
        copy = send(first, last, k)
        copy.start()
        copies.append(copy)
    for copy in copies:
        copy.wait()


def pick_rows(ids, proj, hist, req, halo):
    count = ids.shape[0]
    hidden = proj.shape[1]
    flops = 2 * count * (req + halo) * proj.shape[0] * hidden
    vmem = pl.BlockSpec(memory_space=pltpu.VMEM)
    return pl.pallas_call(
        functools.partial(pick_kernel, req, halo),
        in_specs=[vmem, vmem, vmem],
        out_specs=pl.BlockSpec(memory_space=pltpu.HBM),
        out_shape=jax.ShapeDtypeStruct((count, req + halo, hidden), jnp.bfloat16),
        scratch_shapes=[
            pltpu.VMEM((count, req + halo, hidden), jnp.bfloat16),
            pltpu.SemaphoreType.DMA((len(PICK_CUTS) - 1,)),
        ],
        cost_estimate=pl.CostEstimate(flops=flops, bytes_accessed=3 << 20, transcendentals=0),
        compiler_params=pltpu.CompilerParams(vmem_limit_bytes=24 << 20),
        name="pick_rows",
    )(ids, proj, hist)


def dense_kernel(
    rows_ref, cols_ref, used_ref, tiles_ref, kept_ref, out_ref,
    held_ref, acc_ref, stage_ref, in_sem, out_sem,
):
    slots, side, _ = tiles_ref.shape
    blocks = acc_ref.shape[0] - 1
    kept_blocks = kept_ref.shape[0] // side
    row_blocks, width = out_ref.shape[0] // side, out_ref.shape[1]
    col_blocks = width // side
    chunk = slots // TILE_CHUNKS

    def fetch(c):
        at = pl.ds(c * chunk, chunk)
        return pltpu.make_async_copy(tiles_ref.at[at], held_ref.at[at], in_sem.at[c])

    def flush(r, slot):
        return pltpu.make_async_copy(
            stage_ref.at[slot], out_ref.at[pl.ds(r * side, side)], out_sem.at[slot]
        )

    for c in range(TILE_CHUNKS):
        fetch(c).start()

    @pl.loop(0, blocks)
    def _(b):
        acc_ref[b] = jnp.zeros(acc_ref.shape[1:], jnp.float32)

    @pl.loop(0, TILE_CHUNKS)
    def _(c):
        fetch(c).wait()

        live = jnp.clip(used_ref[0] - c * chunk, 0, chunk)

        @pl.loop(0, (live + TILE_UNROLL - 1) // TILE_UNROLL)
        def _(g):
            for u in range(TILE_UNROLL):
                t = c * chunk + g * TILE_UNROLL + u
                block = rows_ref[t] * col_blocks + cols_ref[t]
                block = jnp.where(t < used_ref[0], block, blocks)
                acc_ref[block] = acc_ref[block] + held_ref[t].astype(jnp.float32)

    @pl.loop(0, row_blocks)
    def _(r):
        slot = lax.rem(r, OUT_SLOTS)

        @pl.when(r >= OUT_SLOTS)
        def _():
            flush(r - OUT_SLOTS, slot).wait()

        for k in range(col_blocks):
            stage_ref[slot, :, k * side : (k + 1) * side] = acc_ref[
                (kept_blocks + r) * col_blocks + k
            ].astype(jnp.bfloat16)
        flush(r, slot).start()

    @pl.loop(0, kept_blocks)
    def _(r):
        at = pl.ds(pl.multiple_of(r * side, side), side)
        for k in range(col_blocks):
            kept_ref[at, k * side : (k + 1) * side] = acc_ref[r * col_blocks + k].astype(
                jnp.bfloat16
            )

    for r in range(row_blocks - OUT_SLOTS, row_blocks):
        flush(r, r % OUT_SLOTS).wait()


def build_dense(tile_rows, tile_cols, tile_count, tile_values, row_blocks, col_blocks):
    slots, side, _ = tile_values.shape
    width = col_blocks * side
    tile_values = pltpu.with_memory_space_constraint(tile_values, pltpu.HBM)
    smem = pl.BlockSpec(memory_space=pltpu.SMEM)
    hbm = pl.BlockSpec(memory_space=pltpu.HBM)
    return pl.pallas_call(
        dense_kernel,
        in_specs=[smem, smem, smem, hbm],
        out_specs=[pl.BlockSpec(memory_space=pltpu.VMEM), hbm],
        out_shape=[
            pltpu.VMEM((KEPT_ROWS, width), jnp.bfloat16),
            jax.ShapeDtypeStruct((row_blocks * side - KEPT_ROWS, width), jnp.bfloat16),
        ],
        scratch_shapes=[
            pltpu.VMEM((slots, side, side), jnp.bfloat16),
            pltpu.VMEM((row_blocks * col_blocks + 1, side, side), jnp.float32),
            pltpu.VMEM((OUT_SLOTS, side, col_blocks * side), jnp.bfloat16),
            pltpu.SemaphoreType.DMA((TILE_CHUNKS,)),
            pltpu.SemaphoreType.DMA((OUT_SLOTS,)),
        ],
        compiler_params=pltpu.CompilerParams(vmem_limit_bytes=56 << 20),
        cost_estimate=pl.CostEstimate(flops=1 << 20, bytes_accessed=30 << 20, transcendentals=0),
        name="build_dense",
    )(tile_rows, tile_cols, tile_count, tile_values)


def combine_kernel(
    req, kept_ref, dense_ref, came_ref, w_ref, out_ref,
    held_ref, source_ref, mixed_ref, stage_ref, in_sem, out_sem,
):
    owners, slots, hidden = came_ref.shape
    nodes = owners * req
    step = ROWS_STEP
    steps = nodes // step

    kept = kept_ref.shape[0]

    def fetch(first, size, k):
        return pltpu.make_async_copy(
            dense_ref.at[pl.ds(first - kept, size)], held_ref.at[pl.ds(first, size)], in_sem.at[k]
        )

    def fetch_step(k):
        return fetch(k * step, step, k)

    start = fetch(kept, step - kept, 0)

    def flush(k):
        at = pl.ds(k * step, step)
        return pltpu.make_async_copy(stage_ref.at[at], out_ref.at[at], out_sem.at[k])

    start.start()
    held_ref[:kept] = kept_ref[...]
    for k in range(1, steps):
        fetch_step(k).start()
    source_ref[:nodes] = came_ref[:, :req, :].reshape(nodes, hidden)
    source_ref[nodes:] = came_ref[:, req:, :].reshape(owners * (slots - req), hidden)

    @pl.loop(0, 3)
    def _(j):
        at = pl.ds(pl.multiple_of(j * 1024, 1024), 1024)
        mixed_ref[at] = jnp.dot(
            source_ref[at], w_ref[...], preferred_element_type=jnp.float32
        ).astype(jnp.bfloat16)

    @pl.loop(0, steps)
    def _(k):
        @pl.when(k == 0)
        def _():
            start.wait()

        @pl.when(k > 0)
        def _():
            fetch_step(k).wait()

        at = pl.ds(pl.multiple_of(k * step, step), step)
        mixed = jnp.dot(held_ref[at], mixed_ref[...], preferred_element_type=jnp.float32)
        own = source_ref[at].astype(jnp.float32)
        stage_ref[at] = jnp.maximum(mixed + own, 0.0).astype(jnp.bfloat16)
        flush(k).start()

    for k in range(steps):
        flush(k).wait()


def combine(kept, dense, came, w_out, req):
    hidden = came.shape[2]
    nodes, width = kept.shape[0] + dense.shape[0], dense.shape[1]
    dense = pltpu.with_memory_space_constraint(dense, pltpu.HBM)
    vmem = pl.BlockSpec(memory_space=pltpu.VMEM)
    hbm = pl.BlockSpec(memory_space=pltpu.HBM)
    return pl.pallas_call(
        functools.partial(combine_kernel, req),
        in_specs=[vmem, hbm, vmem, vmem],
        out_specs=hbm,
        out_shape=jax.ShapeDtypeStruct((nodes, hidden), jnp.bfloat16),
        scratch_shapes=[
            pltpu.VMEM((nodes, width), jnp.bfloat16),
            pltpu.VMEM((width, hidden), jnp.bfloat16),
            pltpu.VMEM((width, hidden), jnp.bfloat16),
            pltpu.VMEM((nodes, hidden), jnp.bfloat16),
            pltpu.SemaphoreType.DMA((nodes // ROWS_STEP,)),
            pltpu.SemaphoreType.DMA((nodes // ROWS_STEP,)),
        ],
        cost_estimate=pl.CostEstimate(
            flops=2 * nodes * width * hidden, bytes_accessed=16 << 20, transcendentals=0
        ),
        compiler_params=pltpu.CompilerParams(vmem_limit_bytes=24 << 20),
        name="combine",
    )(kept, dense, came, w_out)


def on_device(
    features,
    history,
    request_ids,
    request_count,
    halo_ids,
    halo_count,
    tile_values,
    tile_rows,
    tile_cols,
    tile_count,
    w_in,
    w_out,
):
    owners, req = request_ids.shape[1:]
    halo = halo_ids.shape[2]
    side = tile_values.shape[1]
    wanted = pack_ids(request_ids[0].T, halo_ids[0].T, request_count, halo_count)
    asked = lax.all_to_all(wanted, "nodes", split_axis=0, concat_axis=0, tiled=True)
    proj, hist = project(features, history, w_in)
    picked = pick_rows(asked, proj, hist, req, halo)
    picked, tile_count = lax.optimization_barrier((picked, tile_count))
    came = lax.all_to_all(picked, "nodes", split_axis=0, concat_axis=0, tiled=True)
    kept, dense = build_dense(
        tile_rows, tile_cols, tile_count, tile_values,
        owners * req // side, owners * (req + halo) // side,
    )
    return combine(kept, dense, came, w_out, req)


def solution(mesh):
    in_specs = (
        P("nodes", None),
        P("nodes", None),
        P("nodes", None, None),
        P("nodes", None),
        P("nodes", None, None),
        P("nodes", None),
        P("nodes", None, None),
        P("nodes"),
        P("nodes"),
        P("nodes"),
        P(),
        P(),
    )
    out_specs = P("nodes", None)
    return jax.shard_map(
        on_device, mesh=mesh, in_specs=in_specs, out_specs=out_specs, check_vma=False
    )
```

```python
import functools

import jax
import jax.numpy as jnp
from jax import lax
from jax.experimental import pallas as pl
from jax.experimental.pallas import tpu as pltpu
from jax.sharding import PartitionSpec as P

LANES = 128
TILE_CHUNKS = 8
TILE_UNROLL = 4
OUT_SLOTS = 8
PICK_CUTS = (0, 2, 4, 6, 7, 8)
ROWS_STEP = 512
KEPT_ROWS = 256
PROJECT_STEP = 512


def pack_kernel(req_ref, halo_ref, req_count_ref, halo_count_ref, out_ref):
    req = req_ref[...]
    halo = halo_ref[...]
    req_slot = lax.broadcasted_iota(jnp.int32, req.shape, 0)
    halo_slot = lax.broadcasted_iota(jnp.int32, halo.shape, 0)
    req = jnp.where(req_slot < req_count_ref[...], req, -1)
    halo = jnp.where(halo_slot < halo_count_ref[...], halo, -1)
    rest = jnp.full((LANES - req.shape[0] - halo.shape[0], req.shape[1]), -1, jnp.int32)
    out_ref[...] = jnp.concatenate([req, halo, rest], axis=0).T


def pack_ids(req_t, halo_t, req_count, halo_count):
    owners = req_t.shape[1]
    return pl.pallas_call(
        pack_kernel,
        out_specs=pl.BlockSpec(memory_space=pltpu.VMEM),
        out_shape=pltpu.VMEM((owners, LANES), jnp.int32),
        name="pack_ids",
    )(req_t, halo_t, req_count, halo_count)


def project_kernel(
    features_ref, history_ref, w_in_ref, proj_ref, hist_ref,
    rows_ref, old_ref, w_ref, row_sem, old_sem, w_sem,
):
    step = PROJECT_STEP
    steps = proj_ref.shape[0] // step

    def fetch(k):
        at = pl.ds(k * step, step)
        return pltpu.make_async_copy(features_ref.at[at], rows_ref.at[at], row_sem.at[k])

    old = pltpu.make_async_copy(history_ref, old_ref, old_sem)
    weights = pltpu.make_async_copy(w_in_ref, w_ref, w_sem)
    old.start()
    weights.start()
    for k in range(steps):
        fetch(k).start()
    old.wait()
    hist_ref[...] = old_ref[...].astype(jnp.bfloat16)
    weights.wait()

    @pl.loop(0, steps)
    def _(k):
        fetch(k).wait()
        at = pl.ds(pl.multiple_of(k * step, step), step)
        proj_ref[at] = jnp.dot(
            rows_ref[at].astype(jnp.bfloat16), w_ref[...], preferred_element_type=jnp.float32
        ).astype(jnp.bfloat16)


def project(features, history, w_in):
    rows, width = features.shape
    hidden = w_in.shape[1]
    table = pltpu.VMEM((rows, hidden), jnp.bfloat16)
    features = pltpu.with_memory_space_constraint(features, pltpu.HBM)
    history = pltpu.with_memory_space_constraint(history, pltpu.HBM)
    w_in = pltpu.with_memory_space_constraint(w_in, pltpu.HBM)
    vmem = pl.BlockSpec(memory_space=pltpu.VMEM)
    hbm = pl.BlockSpec(memory_space=pltpu.HBM)
    return pl.pallas_call(
        project_kernel,
        in_specs=[hbm, hbm, hbm],
        out_specs=[vmem, vmem],
        out_shape=[table, table],
        scratch_shapes=[
            pltpu.VMEM((rows, width), jnp.float32),
            pltpu.VMEM((rows, hidden), jnp.float32),
            pltpu.VMEM((width, hidden), jnp.bfloat16),
            pltpu.SemaphoreType.DMA((rows // PROJECT_STEP,)),
            pltpu.SemaphoreType.DMA,
            pltpu.SemaphoreType.DMA,
        ],
        cost_estimate=pl.CostEstimate(
            flops=2 * rows * width * hidden, bytes_accessed=5 << 20, transcendentals=0
        ),
        compiler_params=pltpu.CompilerParams(vmem_limit_bytes=60 << 20),
        name="project",
    )(features, history, w_in)


def pick_kernel(req, halo, ids_ref, proj_ref, hist_ref, out_ref, held_ref, sem):
    count = ids_ref.shape[0]
    rows = proj_ref.shape[0]
    turned = ids_ref[...].T

    def pick(table_ref, start, size, first, last):
        wide = jnp.concatenate(
            [
                jnp.broadcast_to(turned[start : start + size, c : c + 1], (size, LANES))
                for c in range(first, last)
            ],
            axis=0,
        )
        high = (wide >> 7).astype(jnp.float32).astype(jnp.bfloat16)
        low = (wide & (LANES - 1)).astype(jnp.float32).astype(jnp.bfloat16)
        lane = lax.broadcasted_iota(jnp.int32, wide.shape, 1)
        lane = lane.astype(jnp.float32).astype(jnp.bfloat16)
        one, zero = jnp.ones_like(low), jnp.zeros_like(low)
        hit = jnp.where(low == lane, one, zero)
        parts = [
            jnp.where(high == jnp.full_like(high, k), hit, zero) for k in range(rows // LANES)
        ]
        picked = jnp.dot(
            jnp.concatenate(parts, axis=1), table_ref[...], preferred_element_type=jnp.float32
        )
        return picked.astype(jnp.bfloat16).reshape(last - first, size, -1)

    def send(first, last, k):
        at = pl.ds(first, last - first)
        return pltpu.make_async_copy(held_ref.at[at], out_ref.at[at], sem.at[k])

    cuts = [count * part // 8 for part in PICK_CUTS]
    copies = []
    for k, (first, last) in enumerate(zip(cuts[:-1], cuts[1:])):
        held_ref[first:last, :req, :] = pick(proj_ref, 0, req, first, last)
        held_ref[first:last, req:, :] = pick(hist_ref, req, halo, first, last)
        copy = send(first, last, k)
        copy.start()
        copies.append(copy)
    for copy in copies:
        copy.wait()


def pick_rows(ids, proj, hist, req, halo):
    count = ids.shape[0]
    hidden = proj.shape[1]
    flops = 2 * count * (req + halo) * proj.shape[0] * hidden
    vmem = pl.BlockSpec(memory_space=pltpu.VMEM)
    return pl.pallas_call(
        functools.partial(pick_kernel, req, halo),
        in_specs=[vmem, vmem, vmem],
        out_specs=pl.BlockSpec(memory_space=pltpu.HBM),
        out_shape=jax.ShapeDtypeStruct((count, req + halo, hidden), jnp.bfloat16),
        scratch_shapes=[
            pltpu.VMEM((count, req + halo, hidden), jnp.bfloat16),
            pltpu.SemaphoreType.DMA((len(PICK_CUTS) - 1,)),
        ],
        cost_estimate=pl.CostEstimate(flops=flops, bytes_accessed=3 << 20, transcendentals=0),
        compiler_params=pltpu.CompilerParams(vmem_limit_bytes=24 << 20),
        name="pick_rows",
    )(ids, proj, hist)


def dense_kernel(
    rows_ref, cols_ref, used_ref, tiles_ref, kept_ref, out_ref,
    held_ref, acc_ref, stage_ref, in_sem, out_sem,
):
    slots, side, _ = tiles_ref.shape
    blocks = acc_ref.shape[0] - 1
    kept_blocks = kept_ref.shape[0] // side
    row_blocks, width = out_ref.shape[0] // side, out_ref.shape[1]
    col_blocks = width // side
    chunk = slots // TILE_CHUNKS

    def fetch(c):
        at = pl.ds(c * chunk, chunk)
        return pltpu.make_async_copy(tiles_ref.at[at], held_ref.at[at], in_sem.at[c])

    def flush(r, slot):
        return pltpu.make_async_copy(
            stage_ref.at[slot], out_ref.at[pl.ds(r * side, side)], out_sem.at[slot]
        )

    for c in range(TILE_CHUNKS):
        fetch(c).start()

    @pl.loop(0, blocks)
    def _(b):
        acc_ref[b] = jnp.zeros(acc_ref.shape[1:], jnp.float32)

    @pl.loop(0, TILE_CHUNKS)
    def _(c):
        fetch(c).wait()

        live = jnp.clip(used_ref[0] - c * chunk, 0, chunk)

        @pl.loop(0, (live + TILE_UNROLL - 1) // TILE_UNROLL)
        def _(g):
            for u in range(TILE_UNROLL):
                t = c * chunk + g * TILE_UNROLL + u
                block = rows_ref[t] * col_blocks + cols_ref[t]
                block = jnp.where(t < used_ref[0], block, blocks)
                acc_ref[block] = acc_ref[block] + held_ref[t].astype(jnp.float32)

    @pl.loop(0, row_blocks)
    def _(r):
        slot = lax.rem(r, OUT_SLOTS)

        @pl.when(r >= OUT_SLOTS)
        def _():
            flush(r - OUT_SLOTS, slot).wait()

        for k in range(col_blocks):
            stage_ref[slot, :, k * side : (k + 1) * side] = acc_ref[
                (kept_blocks + r) * col_blocks + k
            ].astype(jnp.bfloat16)
        flush(r, slot).start()

    @pl.loop(0, kept_blocks)
    def _(r):
        at = pl.ds(pl.multiple_of(r * side, side), side)
        for k in range(col_blocks):
            kept_ref[at, k * side : (k + 1) * side] = acc_ref[r * col_blocks + k].astype(
                jnp.bfloat16
            )

    for r in range(row_blocks - OUT_SLOTS, row_blocks):
        flush(r, r % OUT_SLOTS).wait()


def build_dense(tile_rows, tile_cols, tile_count, tile_values, row_blocks, col_blocks):
    slots, side, _ = tile_values.shape
    width = col_blocks * side
    tile_values = pltpu.with_memory_space_constraint(tile_values, pltpu.HBM)
    smem = pl.BlockSpec(memory_space=pltpu.SMEM)
    hbm = pl.BlockSpec(memory_space=pltpu.HBM)
    return pl.pallas_call(
        dense_kernel,
        in_specs=[smem, smem, smem, hbm],
        out_specs=[pl.BlockSpec(memory_space=pltpu.VMEM), hbm],
        out_shape=[
            pltpu.VMEM((KEPT_ROWS, width), jnp.bfloat16),
            jax.ShapeDtypeStruct((row_blocks * side - KEPT_ROWS, width), jnp.bfloat16),
        ],
        scratch_shapes=[
            pltpu.VMEM((slots, side, side), jnp.bfloat16),
            pltpu.VMEM((row_blocks * col_blocks + 1, side, side), jnp.float32),
            pltpu.VMEM((OUT_SLOTS, side, col_blocks * side), jnp.bfloat16),
            pltpu.SemaphoreType.DMA((TILE_CHUNKS,)),
            pltpu.SemaphoreType.DMA((OUT_SLOTS,)),
        ],
        compiler_params=pltpu.CompilerParams(vmem_limit_bytes=56 << 20),
        cost_estimate=pl.CostEstimate(flops=1 << 20, bytes_accessed=30 << 20, transcendentals=0),
        name="build_dense",
    )(tile_rows, tile_cols, tile_count, tile_values)


def combine_kernel(
    req, kept_ref, dense_ref, came_ref, w_ref, out_ref,
    held_ref, source_ref, mixed_ref, stage_ref, in_sem, out_sem,
):
    owners, slots, hidden = came_ref.shape
    nodes = owners * req
    step = ROWS_STEP
    steps = nodes // step

    kept = kept_ref.shape[0]

    def fetch(first, size, k):
        return pltpu.make_async_copy(
            dense_ref.at[pl.ds(first - kept, size)], held_ref.at[pl.ds(first, size)], in_sem.at[k]
        )

    def fetch_step(k):
        return fetch(k * step, step, k)

    start = fetch(kept, step - kept, 0)

    def flush(k):
        at = pl.ds(k * step, step)
        return pltpu.make_async_copy(stage_ref.at[at], out_ref.at[at], out_sem.at[k])

    start.start()
    for k in range(1, steps):
        fetch_step(k).start()
    held_ref[:kept] = kept_ref[...]
    source_ref[:nodes] = came_ref[:, :req, :].reshape(nodes, hidden)
    source_ref[nodes:] = came_ref[:, req:, :].reshape(owners * (slots - req), hidden)

    @pl.loop(0, 3)
    def _(j):
        at = pl.ds(pl.multiple_of(j * 1024, 1024), 1024)
        mixed_ref[at] = jnp.dot(
            source_ref[at], w_ref[...], preferred_element_type=jnp.float32
        ).astype(jnp.bfloat16)

    @pl.loop(0, steps)
    def _(k):
        @pl.when(k == 0)
        def _():
            start.wait()

        @pl.when(k > 0)
        def _():
            fetch_step(k).wait()

        at = pl.ds(pl.multiple_of(k * step, step), step)
        mixed = jnp.dot(held_ref[at], mixed_ref[...], preferred_element_type=jnp.float32)
        own = source_ref[at].astype(jnp.float32)
        stage_ref[at] = jnp.maximum(mixed + own, 0.0).astype(jnp.bfloat16)
        flush(k).start()

    for k in range(steps):
        flush(k).wait()


def combine(kept, dense, came, w_out, req):
    hidden = came.shape[2]
    nodes, width = kept.shape[0] + dense.shape[0], dense.shape[1]
    dense = pltpu.with_memory_space_constraint(dense, pltpu.HBM)
    vmem = pl.BlockSpec(memory_space=pltpu.VMEM)
    hbm = pl.BlockSpec(memory_space=pltpu.HBM)
    return pl.pallas_call(
        functools.partial(combine_kernel, req),
        in_specs=[vmem, hbm, vmem, vmem],
        out_specs=hbm,
        out_shape=jax.ShapeDtypeStruct((nodes, hidden), jnp.bfloat16),
        scratch_shapes=[
            pltpu.VMEM((nodes, width), jnp.bfloat16),
            pltpu.VMEM((width, hidden), jnp.bfloat16),
            pltpu.VMEM((width, hidden), jnp.bfloat16),
            pltpu.VMEM((nodes, hidden), jnp.bfloat16),
            pltpu.SemaphoreType.DMA((nodes // ROWS_STEP,)),
            pltpu.SemaphoreType.DMA((nodes // ROWS_STEP,)),
        ],
        cost_estimate=pl.CostEstimate(
            flops=2 * nodes * width * hidden, bytes_accessed=16 << 20, transcendentals=0
        ),
        compiler_params=pltpu.CompilerParams(vmem_limit_bytes=24 << 20),
        name="combine",
    )(kept, dense, came, w_out)


def on_device(
    features,
    history,
    request_ids,
    request_count,
    halo_ids,
    halo_count,
    tile_values,
    tile_rows,
    tile_cols,
    tile_count,
    w_in,
    w_out,
):
    owners, req = request_ids.shape[1:]
    halo = halo_ids.shape[2]
    side = tile_values.shape[1]
    wanted = pack_ids(request_ids[0].T, halo_ids[0].T, request_count, halo_count)
    asked = lax.all_to_all(wanted, "nodes", split_axis=0, concat_axis=0, tiled=True)
    proj, hist = project(features, history, w_in)
    picked = pick_rows(asked, proj, hist, req, halo)
    picked, tile_count = lax.optimization_barrier((picked, tile_count))
    came = lax.all_to_all(picked, "nodes", split_axis=0, concat_axis=0, tiled=True)
    kept, dense = build_dense(
        tile_rows, tile_cols, tile_count, tile_values,
        owners * req // side, owners * (req + halo) // side,
    )
    return combine(kept, dense, came, w_out, req)


def solution(mesh):
    in_specs = (
        P("nodes", None),
        P("nodes", None),
        P("nodes", None, None),
        P("nodes", None),
        P("nodes", None, None),
        P("nodes", None),
        P("nodes", None, None),
        P("nodes"),
        P("nodes"),
        P("nodes"),
        P(),
        P(),
    )
    out_specs = P("nodes", None)
    return jax.shard_map(
        on_device, mesh=mesh, in_specs=in_specs, out_specs=out_specs, check_vma=False
    )
```
